32 devices in a mesh: state: 16 (over z, y, x), obs: 2 (over core).
Axes of the slice: x: 2, y: 2, z: 4, core: 2. Of those that a mesh axis runs over, the one named last changes fastest.
Arguments:
- prior_state: bfloat16 [80, 131072], P(None, ('state', 'obs')), may hold values from -6 to 6
- batch_order: int32 [4], replicated, may hold values from 0 to 3, each once
- obs_rows: int32 [4, 16, 512], replicated, may hold values from 0 to 131071
- footprint_weights: float32 [4, 16, 512], replicated, may hold values from 0.1 to 0.6
- obs_values: float32 [4, 512], replicated, may hold values from -8 to 8
- obs_errors: float32 [4, 512], replicated, may hold values from 0.5 to 2
- obs_perturbations: float32 [4, 80, 512], replicated, may hold values from -6 to 6
- target_lists: int32 [4, 8, 4], replicated, may hold values from 0 to 31, as said below
Outputs:
- posterior_state: bfloat16 [80, 131072], P(None, ('state', 'obs'))
The draws below stay inside these ranges and needn't reach their ends.
Inputs may be any that keep to these rules, and one draw needn't show every extreme that they name: `target_lists`: device shard s holds rows s * 4096 to (s + 1) * 4096 - 1; each list names 4 distinct device shards. `batch_order`: each batch appears once.
All inputs are finite; a program needn't handle non-finite values.
Results may differ from the reference program's by a relative error of at most 0.008.
Values sent between devices are 32-bit elements; how exact they have to be, the bound alone decides.
No kernel may reach another device: no remote copies, remote signals or barrier semaphores. Data moves between devices by JAX's collectives and lax.ppermute only.
A program may use at most 64 MiB of HBM per device.

```python
import math
import jax
import jax.numpy as jnp
from jax import lax

M = 80
NB = 4
NOBS = 512
NK = 8
KR = 16
RD = 4096
ROWS = 131072
OBK = 64
NT = 4


def target_centres(key):
    return jax.random.randint(jax.random.fold_in(key, 11), (NB, NK), NT // 2, ROWS // RD - NT // 2).astype(jnp.int32)


def draw_target_lists(key, part):
    centres = target_centres(key)
    half_span = NT // 2
    offsets = jnp.concatenate([jnp.arange(-half_span + 1, 0), jnp.arange(1, half_span + 1)]).astype(jnp.int32)
    scores = jax.random.randint(jax.random.fold_in(key, 12), (NB, NK, NT - 1), 0, 1 << 20) * NT + jnp.arange(NT - 1)
    ordering = jnp.argsort(scores, axis=-1, stable=True)
    shuffled = offsets[ordering]
    offsets_all = jnp.concatenate([jnp.zeros((NB, NK, 1), jnp.int32), shuffled], axis=-1)
    return (centres[:, :, None] + offsets_all).astype(jnp.int32)


def draw_obs_rows(key, part):
    centres = target_centres(key)
    reach_rows = NT * RD // 2
    shifts = jax.random.randint(jax.random.fold_in(key, 13), (NB, KR, NOBS), -reach_rows, reach_rows)
    block_ids = jnp.arange(NOBS) // OBK
    middle = centres[:, block_ids] * RD + RD // 2
    near_rows = middle[:, None, :] + shifts
    far_shift = jax.random.randint(jax.random.fold_in(key, 14), (NB, 1, NOBS), -(RD // 2), RD // 2)
    far_rows = (middle[:, None, :] + ROWS // 2 + far_shift) % ROWS
    return jnp.concatenate([near_rows[:, :KR - 1, :], far_rows], axis=1).astype(jnp.int32)


def block_levels(own_key, extent, pieces, smallest, top_value):
    loudness = 1.0
    for axis_at, shards_of in pieces:
        heights = jax.random.uniform(jax.random.fold_in(jax.random.fold_in(own_key, 6), axis_at), (shards_of,), jnp.float32, smallest / len(pieces), top_value / len(pieces))
        loudness = loudness * jnp.repeat(jnp.exp(heights), extent[axis_at] // shards_of).reshape((-1,) + (1,) * (len(extent) - 1 - axis_at))
    return loudness


def gaussian(key, shape, scale, bound, split=(), kind=jnp.bfloat16):
    result = jax.random.normal(key, shape, jnp.float32) * scale
    if len(split) > 0:
        result = block_levels(key, shape, split, -0.22, 0.18) * result
    return jnp.clip(result, min=-bound, max=bound).astype(kind)


def setup_inputs(seed: int = 0) -> dict:
    arg_keys = jax.random.split(jax.random.key(seed), 9)
    prior_state = gaussian(arg_keys[0], (M, ROWS), 1.0, 6.0, ((1, 32),))
    batch_order = jax.random.permutation(arg_keys[1], NB).astype(jnp.int32)
    obs_rows = draw_obs_rows(jax.random.fold_in(arg_keys[8], 71), 0)
    footprint_weights = jnp.clip(jax.random.uniform(arg_keys[3], (NB, KR, NOBS), jnp.float32, 0.1, 0.6), 0.1, 0.6)
    obs_values = gaussian(arg_keys[4], (NB, NOBS), 1.5, 8.0, (), jnp.float32)
    obs_errors = jnp.clip(jnp.exp(jax.random.uniform(arg_keys[5], (NB, NOBS), jnp.float32, math.log(0.5), math.log(2.0))), 0.5, 2.0)
    obs_perturbations = gaussian(arg_keys[6], (NB, M, NOBS), 1.0, 6.0, (), jnp.float32)
    target_lists = draw_target_lists(jax.random.fold_in(arg_keys[8], 71), 0)
    return {"prior_state": prior_state, "batch_order": batch_order, "obs_rows": obs_rows, "footprint_weights": footprint_weights, "obs_values": obs_values, "obs_errors": obs_errors, "obs_perturbations": obs_perturbations, "target_lists": target_lists}


def ensemble_transforms(ensemble, values, errors, perturb):
    members = ensemble.shape[0]
    spread_scale = math.sqrt(members - 1)
    blocks = ensemble.reshape(members, -1, OBK).transpose(1, 0, 2)
    errors_block = errors.reshape(-1, OBK)[:, None, :]
    observed = values.reshape(-1, OBK)[:, None, :]
    perturbed = perturb.reshape(members, -1, OBK).transpose(1, 0, 2)
    spread = (blocks - lax.optimization_barrier(jnp.mean(blocks, axis=1, keepdims=True))) / (errors_block * spread_scale)
    misfit = (observed + errors_block * perturbed - blocks) / errors_block
    system = jnp.eye(members, dtype=ensemble.dtype)[None] + jnp.einsum('kmp,knp->kmn', spread, spread, precision=lax.Precision.HIGHEST)
    right_side = jnp.einsum('kmp,knp->kmn', spread, misfit, precision=lax.Precision.HIGHEST)
    factor = jnp.linalg.cholesky(system)
    partial_solve = jax.scipy.linalg.solve_triangular(factor, right_side, lower=True)
    solved = jax.scipy.linalg.solve_triangular(factor, partial_solve, lower=True, trans=1)
    return jnp.swapaxes(solved, 1, 2) / spread_scale

def reference(prior_state, batch_order, obs_rows, footprint_weights, obs_values, obs_errors, obs_perturbations, target_lists):
    reach_span = target_lists.shape[2]
    reach_rows = reach_span * RD // 2
    current = prior_state
    for step_index in range(NB):
        batch_id = batch_order[step_index]
        batch_rows = obs_rows[batch_id]
        picked_rows = jnp.take(current, batch_rows, axis=1).astype(jnp.float32)
        ensemble = lax.optimization_barrier(jnp.sum(picked_rows * footprint_weights[batch_id][None], axis=1))
        weights = ensemble_transforms(ensemble, obs_values[batch_id], obs_errors[batch_id], obs_perturbations[batch_id])
        lists = target_lists[batch_id]
        frozen = current

        def add_one(flat_index, updated):
            block_id = flat_index // reach_span
            slot_id = flat_index % reach_span
            begin = (lists[block_id, slot_id] * RD).astype(jnp.int32)
            piece = lax.dynamic_slice_in_dim(frozen, begin, RD, 1).astype(jnp.float32)
            anomalies = piece - lax.optimization_barrier(jnp.mean(piece, axis=0, keepdims=True))
            positions = begin + jnp.arange(RD, dtype=jnp.int32)
            centre = lists[block_id, 0] * RD + RD // 2
            distance = jnp.abs(positions - centre).astype(jnp.float32) / reach_rows
            taper = jnp.maximum(0.0, 1.0 - distance) ** 2
            increment = jnp.dot(weights[block_id], anomalies * taper[None, :], precision=lax.Precision.HIGHEST)
            before = lax.dynamic_slice_in_dim(updated, begin, RD, 1)
            return lax.dynamic_update_slice_in_dim(updated, before + increment, begin, 1)
        updated = lax.fori_loop(0, NK * reach_span, add_one, frozen.astype(jnp.float32))
        current = updated.astype(jnp.bfloat16)
    return current
```

```python
import functools
import math

import jax
import jax.numpy as jnp
from jax import lax
from jax.experimental import pallas as pl
from jax.experimental.pallas import tpu as pltpu
from jax.sharding import PartitionSpec as P

OBK = 64
LO = 256
GROUP = 2
HIGHEST = lax.Precision.HIGHEST


def observe_into(state_ref, tiles_ref, rows_ref, weights_ref, part_ref, keep_ref, send_ref, active, base, half):
    blocks = part_ref.shape[0]
    members = state_ref.shape[0]
    tiles = state_ref.shape[1] // LO
    pairs = rows_ref.shape[-1]
    for tile in range(tiles):
        tiles_ref[tile] = state_ref[:, tile * LO : (tile + 1) * LO]

    def one_block(block_id, carry):
        @pl.when(active(block_id) == 0)
        def _():
            part_ref[block_id] = jnp.zeros((members, 2 * OBK), jnp.float32)

        @pl.when(active(block_id) != 0)
        def _():
            stacked = tiles_ref[...].reshape(tiles * members, LO)
            total = jnp.zeros((members, 2 * OBK), jnp.float32)
            for start in range(0, pairs, LO):
                rows = rows_ref[0, pl.ds(block_id, 1), start : start + LO] - base
                weights = weights_ref[0, pl.ds(block_id, 1), start : start + LO]
                low = rows & (LO - 1)
                high = rows >> (LO.bit_length() - 1)
                chosen = (lax.broadcasted_iota(jnp.int32, (LO, LO), 0) == low).astype(jnp.float32)
                picked = jnp.dot(stacked, chosen.astype(jnp.bfloat16), preferred_element_type=jnp.float32)
                acc = jnp.zeros((members, LO), jnp.float32)
                for tile in range(tiles):
                    scale = jnp.where(high == tile, weights, 0.0)
                    acc = acc + picked[tile * members : (tile + 1) * members] * scale
                for lane in range(0, LO, 2 * OBK):
                    total = total + acc[:, lane : lane + 2 * OBK]
            part_ref[block_id] = total + pltpu.roll(total, OBK, 1)

        return carry

    lax.fori_loop(0, blocks, one_block, 0)
    low_lane = lax.broadcasted_iota(jnp.int32, (members, 2 * OBK), 1) < OBK
    quarter = blocks // 4
    for slot in range(quarter):
        for out_ref, side in ((keep_ref, half), (send_ref, 1 - half)):
            first = 2 * (side * quarter + slot)
            out_ref[slot] = jnp.where(low_lane, part_ref[first], part_ref[first + 1])


def block_transforms(spreads, misfits, scale):
    obs = spreads[0].shape[0]
    count = len(spreads)
    eye = (
        lax.broadcasted_iota(jnp.int32, (obs, obs), 0) == lax.broadcasted_iota(jnp.int32, (obs, obs), 1)
    ).astype(jnp.float32)
    sublane = lax.broadcasted_iota(jnp.int32, (8, 1), 0)
    nt = (((1,), (1,)), ((), ()))
    tn = (((0,), (0,)), ((), ()))
    split = lambda x: [x[i : i + 8] for i in range(0, obs, 8)]
    system = [
        split(eye + lax.dot_general(s, s, nt, precision=HIGHEST, preferred_element_type=jnp.float32)) for s in spreads
    ]
    right = [split(s) for s in spreads]
    left = [split(m) for m in misfits]
    scaled = [[] for _ in range(count)]
    for k in range(obs):
        at, sub = divmod(k, 8)
        for g in range(count):
            pivot = system[g][at][sub : sub + 1, k : k + 1]
            inverse = 1.0 / pivot
            row_s = system[g][at][sub : sub + 1] * inverse
            row_r = right[g][at][sub : sub + 1] * inverse
            row_l = left[g][at][sub : sub + 1] * inverse
            scaled[g].append(row_r)
            for i in range(at, obs // 8):
                if i == at and sub == 7:
                    continue
                column = system[g][i][:, k : k + 1]
                if i == at:
                    column = jnp.where(sublane > sub, column, 0.0)
                system[g][i] = system[g][i] - column * row_s
                right[g][i] = right[g][i] - column * row_r
                left[g][i] = left[g][i] - column * row_l
    results = []
    for g in range(count):
        a = jnp.concatenate(left[g], axis=0)
        b = jnp.concatenate(scaled[g], axis=0)
        results.append(
            lax.dot_general(a, b, tn, precision=HIGHEST, preferred_element_type=jnp.float32) * (1.0 / scale)
        )
    return results


def first_kernel(blocks, meta_ref, state_ref, rows_ref, weights_ref, keep_ref, send_ref, tiles_ref, part_ref):
    base = meta_ref[0] * state_ref.shape[1]
    half = meta_ref[1]
    batch = meta_ref[2]
    active = lambda block_id: meta_ref[8 + batch * blocks + block_id]
    observe_into(state_ref, tiles_ref, rows_ref, weights_ref, part_ref, keep_ref, send_ref, active, base, half)


def step_kernel(
    blocks,
    span,
    step,
    last,
    meta_ref,
    state_ref,
    own_ref,
    other_ref,
    values_ref,
    errors_ref,
    perturb_ref,
    *rest,
):
    if last:
        new_ref, ens_ref, acc_ref, order_ref = rest
    else:
        rows_ref, weights_ref, new_ref, keep_ref, send_ref, ens_ref, acc_ref, order_ref, tiles_ref, part_ref = rest
    members, rows_dev = state_ref.shape
    shard_id = meta_ref[0]
    half = meta_ref[1]
    base = shard_id * rows_dev
    nb = 4
    batch = meta_ref[2 + step]
    targets = 8 + (nb + batch) * blocks
    centres = 8 + (2 * nb + batch) * blocks
    quarter = blocks // 4
    scale = math.sqrt(members - 1)
    reach_rows = span * rows_dev // 2

    ens_ref[pl.ds(half * quarter, quarter)] = own_ref[...]
    ens_ref[pl.ds((1 - half) * quarter, quarter)] = other_ref[...]
    acc_ref[...] = state_ref[...].astype(jnp.float32)

    def scan(block_id, found):
        order_ref[found] = block_id
        return found + (meta_ref[targets + block_id] != 0).astype(jnp.int32)

    found = lax.fori_loop(0, blocks, scan, jnp.int32(0))

    def one_group(group, carry):
        spreads, misfits, ids = [], [], []
        pad = jnp.zeros((128 - members, 2 * OBK), jnp.float32)
        for slot in range(GROUP):
            place = group * GROUP + slot
            block_id = order_ref[jnp.minimum(place, found - 1)]
            pair = block_id // 2
            odd = block_id - 2 * pair
            ens = ens_ref[pair]
            lanes = pl.ds(pl.multiple_of(pair * 2 * OBK, 2 * OBK), 2 * OBK)
            error = errors_ref[0, :, lanes]
            value = values_ref[0, :, lanes]
            pert = perturb_ref[0, :, lanes]
            mean = jnp.sum(ens, axis=0, keepdims=True) * (1.0 / members)
            spread = (ens - mean) / (error * scale)
            misfit = (value + error * pert - ens) / error
            turn = lambda x: jnp.concatenate([x, pad], axis=0).T
            pick = lambda x: jnp.where(odd == 1, x[OBK:], x[:OBK])
            spreads.append(pick(turn(spread)))
            misfits.append(pick(turn(misfit)))
            ids.append((place, block_id))
        transforms = block_transforms(spreads, misfits, scale)
        for slot in range(GROUP):
            place, block_id = ids[slot]
            transform = transforms[slot][:members]
            centred = transform - jnp.sum(transform, axis=1, keepdims=True) * (1.0 / members)
            centred = centred[:, :members]
            coarse = centred.astype(jnp.bfloat16)
            fine = (centred - coarse.astype(jnp.float32)).astype(jnp.bfloat16)
            both = jnp.concatenate([coarse, fine], axis=0)

            @pl.when(place < found)
            def _():
                centre = meta_ref[centres + block_id]
                for start in range(0, rows_dev, LO):
                    cols = slice(start, start + LO)
                    product = jnp.dot(both, state_ref[:, cols], preferred_element_type=jnp.float32)
                    positions = base + start + lax.broadcasted_iota(jnp.int32, (1, LO), 1)
                    distance = jnp.abs(positions - centre).astype(jnp.float32) / reach_rows
                    hat = jnp.maximum(0.0, 1.0 - distance)
                    acc_ref[:, cols] += (product[:members] + product[members:]) * (hat * hat)

        return carry

    lax.fori_loop(0, (found + GROUP - 1) // GROUP, one_group, 0)
    new_ref[...] = acc_ref[...].astype(jnp.bfloat16)
    if not last:
        following = meta_ref[2 + step + 1]
        active = lambda block_id: meta_ref[8 + following * blocks + block_id]
        observe_into(new_ref, tiles_ref, rows_ref, weights_ref, part_ref, keep_ref, send_ref, active, base, half)


def shards(
    n_state,
    n_obs,
    prior_state,
    batch_order,
    obs_rows,
    footprint_weights,
    obs_values,
    obs_errors,
    obs_perturbations,
    target_lists,
):
    members, rows_dev = prior_state.shape
    nb, blocks, span = target_lists.shape
    reads = obs_rows.shape[1]
    nobs = obs_rows.shape[2]
    shard_id = lax.axis_index(("state", "obs"))
    half = lax.axis_index("obs") % 2
    pairs = reads * OBK
    to_pairs = lambda x: x.reshape(nb, reads, blocks, OBK).transpose(0, 2, 1, 3).reshape(nb, blocks, pairs)
    rows = to_pairs(obs_rows)
    weights = to_pairs(footprint_weights)
    owners = obs_rows.reshape(nb, reads, blocks, OBK) // rows_dev
    touched = jnp.any(owners == shard_id, axis=(1, 3)).astype(jnp.int32)
    targeted = jnp.any(target_lists == shard_id, axis=2).astype(jnp.int32)
    centres = target_lists[:, :, 0] * rows_dev + rows_dev // 2
    head = jnp.zeros((8,), jnp.int32).at[0].set(shard_id).at[1].set(half)
    head = lax.dynamic_update_slice(head, batch_order, (2,))
    meta = jnp.concatenate([head, touched.reshape(-1), targeted.reshape(-1), centres.reshape(-1)])

    quarter = blocks // 4
    half_shape = jax.ShapeDtypeStruct((quarter, members, 2 * OBK), jnp.float32)
    state_shape = jax.ShapeDtypeStruct((members, rows_dev), jnp.bfloat16)
    whole2 = lambda i, m: (0, 0)
    whole3 = lambda i, m: (0, 0, 0)
    state_spec = pl.BlockSpec((members, rows_dev), whole2)
    half_spec = pl.BlockSpec((quarter, members, 2 * OBK), whole3)
    params = pltpu.CompilerParams(vmem_limit_bytes=48 * 1024 * 1024)
    tile_scratch = [
        pltpu.VMEM((rows_dev // LO, members, LO), jnp.bfloat16),
        pltpu.VMEM((blocks, members, 2 * OBK), jnp.float32),
    ]

    def pair_specs(step):
        pick = lambda i, m: (m[2 + step], 0, 0)
        return [pl.BlockSpec((1, blocks, pairs), pick)] * 2

    def reduce_all(keep, send):
        flip = lambda x, axis, bit, size: lax.ppermute(x, axis, [(j, j ^ bit) for j in range(size)])
        total = keep + flip(send, "obs", 1, n_obs)
        bit = 2
        while bit < n_obs:
            total = total + flip(total, "obs", bit, n_obs)
            bit *= 2
        bit = 1
        while bit < n_state:
            total = total + flip(total, "state", bit, n_state)
            bit *= 2
        return total, flip(total, "obs", 1, n_obs)

    keep, send = pl.pallas_call(
        functools.partial(first_kernel, blocks),
        out_shape=(half_shape, half_shape),
        grid_spec=pltpu.PrefetchScalarGridSpec(
            num_scalar_prefetch=1,
            grid=(1,),
            in_specs=[state_spec] + pair_specs(0),
            out_specs=(half_spec, half_spec),
            scratch_shapes=tile_scratch,
        ),
        compiler_params=params,
        name="observe",
    )(meta, prior_state, rows, weights)
    current = prior_state
    for step in range(nb):
        last = step == nb - 1
        own, other = reduce_all(keep, send)
        pick = lambda i, m, step=step: (m[2 + step], 0, 0)
        in_specs = [
            state_spec,
            half_spec,
            half_spec,
            pl.BlockSpec((1, 1, nobs), pick),
            pl.BlockSpec((1, 1, nobs), pick),
            pl.BlockSpec((1, members, nobs), pick),
        ]
        args = [meta, current, own, other, obs_values[:, None, :], obs_errors[:, None, :], obs_perturbations]
        scratch = [
            pltpu.VMEM((2 * quarter, members, 2 * OBK), jnp.float32),
            pltpu.VMEM((members, rows_dev), jnp.float32),
            pltpu.SMEM((blocks + 1,), jnp.int32),
        ]
        if not last:
            in_specs += pair_specs(step + 1)
            args += [rows, weights]
            scratch += tile_scratch
        outs = pl.pallas_call(
            functools.partial(step_kernel, blocks, span, step, last),
            out_shape=(state_shape,) if last else (state_shape, half_shape, half_shape),
            grid_spec=pltpu.PrefetchScalarGridSpec(
                num_scalar_prefetch=1,
                grid=(1,),
                in_specs=in_specs,
                out_specs=(state_spec,) if last else (state_spec, half_spec, half_spec),
                scratch_shapes=scratch,
            ),
            compiler_params=params,
            name="last_update" if last else "update_observe",
        )(*args)
        current = outs[0]
        if not last:
            keep, send = outs[1:]
    return current


def solution(mesh):
    return jax.shard_map(
        functools.partial(shards, mesh.shape["state"], mesh.shape["obs"]),
        mesh=mesh,
        in_specs=(P(None, ("state", "obs")), P(), P(), P(), P(), P(), P(), P()),
        out_specs=P(None, ("state", "obs")),
        check_vma=False,
    )
```

```python
import functools
import math

import jax
import jax.numpy as jnp
from jax import lax
from jax.experimental import pallas as pl
from jax.experimental.pallas import tpu as pltpu
from jax.sharding import PartitionSpec as P

OBK = 64
LANES = 128
LO = 256
GROUP = 4
HOPS = (2, 2)
HIGHEST = lax.Precision.HIGHEST
NT = (((1,), (1,)), ((), ()))
TN = (((0,), (0,)), ((), ()))


def touched_blocks(rows_ref, base, rows_dev, flags_ref):
    batches, _, nobs = rows_ref.shape
    lane = lax.broadcasted_iota(jnp.int32, (1, LANES), 1)
    bits = 16
    words = [jnp.zeros((1, 1), jnp.float32) for _ in range(batches * nobs // (OBK * bits))]
    place = 0
    for batch in range(batches):
        local = rows_ref[batch] - base
        inside = jnp.where((local >= 0) & (local < rows_dev), 1.0, 0.0)
        hits = jnp.max(inside, axis=0, keepdims=True)
        for tile in range(nobs // LANES):
            part = hits[:, tile * LANES : (tile + 1) * LANES]
            for side in (lane < OBK, lane >= OBK):
                any_hit = jnp.max(jnp.where(side, part, 0.0), axis=1, keepdims=True)
                words[place // bits] = words[place // bits] + any_hit * float(1 << (place % bits))
                place += 1
    for at, word in enumerate(words):
        packed = word[0, 0].astype(jnp.int32)
        for bit in range(bits):
            flags_ref[at * bits + bit] = (packed >> bit) & 1


def observe_into(tiles_ref, rows_ref, weights_ref, slot, part_ref, keep_ref, send_ref, active, base, half):
    blocks = part_ref.shape[0]
    tiles, members, _ = tiles_ref.shape
    reads = rows_ref.shape[1]
    fold = reads // 2
    lane = lax.broadcasted_iota(jnp.int32, (fold, LANES), 1)

    def one_block(block_id, carry):
        @pl.when(active(block_id) == 0)
        def _():
            part_ref[block_id] = jnp.zeros((members, LANES), jnp.float32)

        @pl.when(active(block_id) != 0)
        def _():
            pair = block_id // 2
            odd = block_id - 2 * pair
            lanes = pl.ds(pl.multiple_of(pair * LANES, LANES), LANES)

            def folded(ref):
                top = ref[slot, :fold, lanes]
                bottom = ref[slot, fold:, lanes]
                even = jnp.where(lane < OBK, top, pltpu.roll(bottom, OBK, 1))
                other = jnp.where(lane < OBK, pltpu.roll(top, OBK, 1), bottom)
                return jnp.where(odd == 1, other, even)

            rows = folded(rows_ref) - base
            weights = folded(weights_ref)
            stacked = tiles_ref[...].reshape(tiles * members, LO)
            total = jnp.zeros((members, LANES), jnp.float32)
            for read in range(0, fold, 2):
                pick = lambda x: jnp.concatenate([x[read : read + 1], x[read + 1 : read + 2]], axis=1)
                row = pick(rows)
                weight = pick(weights)
                low = row & (LO - 1)
                high = row >> (LO.bit_length() - 1)
                chosen = (lax.broadcasted_iota(jnp.int32, (LO, LO), 0) == low).astype(jnp.float32)
                picked = jnp.dot(stacked, chosen.astype(jnp.bfloat16), preferred_element_type=jnp.float32)
                acc = jnp.zeros((members, LO), jnp.float32)
                for tile in range(tiles):
                    scale = jnp.where(high == tile, weight, 0.0)
                    acc = acc + picked[tile * members : (tile + 1) * members] * scale
                total = total + (acc[:, :LANES] + acc[:, LANES:])
            part_ref[block_id] = total + pltpu.roll(total, OBK, 1)

        return carry

    lax.fori_loop(0, blocks, one_block, 0)
    low_lane = lax.broadcasted_iota(jnp.int32, (members, LANES), 1) < OBK
    quarter = blocks // 4
    for at in range(quarter):
        for out_ref, side in ((keep_ref, half), (send_ref, 1 - half)):
            first = 2 * (side * quarter + at)
            out_ref[at] = jnp.where(low_lane, part_ref[first], part_ref[first + 1])


def block_transforms(spreads, misfits, scale):
    obs = spreads[0].shape[0]
    tiles = obs // 8
    groups = range(len(spreads))
    wide = (8, LANES)
    eye = lax.broadcasted_iota(jnp.int32, (obs, obs), 0) == lax.broadcasted_iota(jnp.int32, (obs, obs), 1)
    sublane = lax.broadcasted_iota(jnp.int32, wide, 0)
    split = lambda x: [x[i : i + 8] for i in range(0, obs, 8)]
    row = lambda x, j: jnp.broadcast_to(x[j : j + 1], (8, x.shape[1]))
    system = [
        split(eye.astype(jnp.float32) + lax.dot_general(s, s, NT, precision=HIGHEST, preferred_element_type=jnp.float32))
        for s in spreads
    ]
    right = [split(s) for s in spreads]
    left = [split(m) for m in misfits]
    scaled = [[] for _ in groups]
    for p in range(tiles):
        columns = [
            [[jnp.broadcast_to(system[g][i][:, 8 * p + j : 8 * p + j + 1], wide) for i in range(p, tiles)] for j in range(8)]
            for g in groups
        ]
        factors = [[] for _ in groups]
        inverses = [[] for _ in groups]
        for j in range(8):
            for g in groups:
                panel = columns[g]
                inverse = 1.0 / row(panel[j][0], j)
                factor = [x * inverse for x in panel[j]]
                factor[0] = jnp.where(sublane > j, factor[0], 0.0)
                for k in range(j + 1, 8):
                    pivot_row = row(panel[k][0], j)
                    panel[k] = [x - f * pivot_row for x, f in zip(panel[k], factor)]
                factors[g].append(factor)
                inverses[g].append(inverse)
        for j in range(8):
            for g in groups:
                row_s, row_r, row_l = row(system[g][p], j), row(right[g][p], j), row(left[g][p], j)
                scaled[g].append(right[g][p][j : j + 1] * inverses[g][j][j : j + 1])
                for i in range(p, tiles):
                    if i == p and j == 7:
                        continue
                    factor = factors[g][j][i - p]
                    if i > p or j < 7:
                        system[g][i] = system[g][i] - factor[:, :obs] * row_s
                    right[g][i] = right[g][i] - factor * row_r
                    left[g][i] = left[g][i] - factor * row_l
    return [
        lax.dot_general(
            jnp.concatenate(left[g], axis=0),
            jnp.concatenate(scaled[g], axis=0),
            TN,
            precision=HIGHEST,
            preferred_element_type=jnp.float32,
        )
        * (1.0 / scale)
        for g in groups
    ]


def first_kernel(
    order_hbm,
    state_hbm,
    rows_hbm,
    weights_hbm,
    keep_ref,
    send_ref,
    flags_ref,
    order_ref,
    state_ref,
    rows_ref,
    weights_ref,
    tiles_ref,
    part_ref,
    sems,
):
    pairs = ((rows_hbm, rows_ref), (order_hbm, order_ref), (state_hbm, state_ref), (weights_hbm, weights_ref))
    copies = [pltpu.make_async_copy(a, b, sems.at[i]) for i, (a, b) in enumerate(pairs)]
    for copy in copies:
        copy.start()
    blocks = part_ref.shape[0]
    rows_dev = state_ref.shape[1]
    base = lax.axis_index(("state", "obs")) * rows_dev
    half = lax.axis_index("obs") % 2
    copies[0].wait()
    touched_blocks(rows_ref, base, rows_dev, flags_ref)
    for copy in copies[1:]:
        copy.wait()
    for tile in range(rows_dev // LO):
        tiles_ref[tile] = state_ref[:, tile * LO : (tile + 1) * LO]
    batch = order_ref[0]
    active = lambda block_id: flags_ref[batch * blocks + block_id]
    observe_into(tiles_ref, rows_ref, weights_ref, batch, part_ref, keep_ref, send_ref, active, base, half)


def step_kernel(
    blocks,
    span,
    step,
    last,
    order_ref,
    lists_ref,
    flags_ref,
    state_ref,
    own_ref,
    other_ref,
    values_ref,
    errors_ref,
    perturb_ref,
    *rest,
):
    if last:
        new_ref, ens_ref, acc_ref, named_ref = rest
    else:
        rows_ref, weights_ref, new_ref, keep_ref, send_ref, ens_ref, acc_ref, named_ref = rest[:8]
        tiles_ref, part_ref = rest[8:]
    members, rows_dev = state_ref.shape
    shard_id = lax.axis_index(("state", "obs"))
    half = lax.axis_index("obs") % 2
    base = shard_id * rows_dev
    batch = order_ref[step]
    quarter = blocks // 4
    scale = math.sqrt(members - 1)
    reach_rows = span * rows_dev // 2

    ens_ref[pl.ds(half * quarter, quarter)] = own_ref[...]
    ens_ref[pl.ds((1 - half) * quarter, quarter)] = other_ref[...]

    def scan(block_id, found):
        begin = (batch * blocks + block_id) * span
        look = lambda slot, hit: hit | (lists_ref[begin + slot] == shard_id).astype(jnp.int32)
        named_ref[found] = block_id
        return found + lax.fori_loop(0, span, look, jnp.int32(0))

    found = lax.fori_loop(0, blocks, scan, jnp.int32(0))

    def transposed(place):
        block_id = named_ref[place]
        pair = block_id // 2
        odd = block_id - 2 * pair
        ens = ens_ref[pair]
        lanes = pl.ds(pl.multiple_of(pair * LANES, LANES), LANES)
        mine = lax.broadcasted_iota(jnp.int32, (values_ref.shape[0], LANES), 0) == batch
        of_batch = lambda ref: jnp.sum(jnp.where(mine, ref[:, lanes], 0.0), axis=0, keepdims=True)
        error = of_batch(errors_ref)
        value = of_batch(values_ref)
        pert = perturb_ref[0, :, lanes]
        mean = jnp.sum(ens, axis=0, keepdims=True) * (1.0 / members)
        spread = (ens - mean) / (error * scale)
        misfit = (value + error * pert - ens) / error
        pad = jnp.zeros((LANES - members, LANES), jnp.float32)
        turn = lambda x: jnp.concatenate([x, pad], axis=0).T
        pick = lambda x: jnp.where(odd == 1, x[OBK:], x[:OBK])
        return pick(turn(spread)), pick(turn(misfit))

    def put(tile, value):
        value = value.astype(jnp.bfloat16)
        new_ref[:, tile * LO : (tile + 1) * LO] = value
        if not last:
            tiles_ref[tile] = value

    tiles = rows_dev // LO

    @pl.when(found == 0)
    def _():
        for tile in range(tiles):
            put(tile, state_ref[:, tile * LO : (tile + 1) * LO])

    def update(places, results, more):
        pieces, centres = [], []
        for place, result in zip(places, results):
            result = result[:members]
            centred = result - jnp.sum(result, axis=1, keepdims=True) * (1.0 / members)
            centred = centred[:, :members]
            coarse = centred.astype(jnp.bfloat16)
            fine = (centred - coarse.astype(jnp.float32)).astype(jnp.bfloat16)
            pieces += [coarse, fine]
            centres.append(lists_ref[(batch * blocks + named_ref[place]) * span] * rows_dev + rows_dev // 2)
        pieces = jnp.concatenate(pieces, axis=0)
        for tile in range(tiles):
            cols = slice(tile * LO, (tile + 1) * LO)
            product = jnp.dot(pieces, state_ref[:, cols], preferred_element_type=jnp.float32)
            value = acc_ref[:, cols] if more else state_ref[:, cols].astype(jnp.float32)
            positions = base + tile * LO + lax.broadcasted_iota(jnp.int32, (1, LO), 1)
            for slot, centre in enumerate(centres):
                distance = jnp.abs(positions - centre).astype(jnp.float32) / reach_rows
                hat = jnp.maximum(0.0, 1.0 - distance)
                at = 2 * slot * members
                value = value + (product[at : at + members] + product[at + members : at + 2 * members]) * (hat * hat)
            if more or len(places) == GROUP:
                acc_ref[:, cols] = value
            put(tile, value)

    def one_group(size, first, more):
        places = [first + slot for slot in range(size)]
        sides = [transposed(place) for place in places]
        update(places, block_transforms([s for s, _ in sides], [m for _, m in sides], scale), more)

    for size in range(2, GROUP):
        pl.when(found == size)(functools.partial(one_group, size, 0, False))
    pl.when(found >= GROUP)(functools.partial(one_group, GROUP, 0, False))

    @pl.when(found == 1)
    def _():
        acc_ref[...] = state_ref[...].astype(jnp.float32)

    @pl.when((found == 1) | (found > GROUP))
    def _():
        def single(place, carry):
            one_group(1, place, True)
            return carry

        lax.fori_loop(jnp.where(found == 1, 0, GROUP), found, single, 0)

    if not last:
        following = order_ref[step + 1] * blocks
        active = lambda block_id: flags_ref[following + block_id]
        observe_into(tiles_ref, rows_ref, weights_ref, 0, part_ref, keep_ref, send_ref, active, base, half)


def hop(x, axis, flips, size):
    send = lambda bits: lax.ppermute(x, axis, [(j, j ^ bits) for j in range(size)])
    if len(flips) == 1:
        return x + send(flips[0])
    one, two = flips
    a, b, c = send(one), send(two), send(one | two)
    return (x + a) + (b + c)


def shards(
    n_state,
    n_obs,
    prior_state,
    batch_order,
    obs_rows,
    footprint_weights,
    obs_values,
    obs_errors,
    obs_perturbations,
    target_lists,
):
    members, rows_dev = prior_state.shape
    nb, blocks, span = target_lists.shape
    reads, nobs = obs_rows.shape[1:]
    quarter = blocks // 4
    lists = target_lists.reshape(-1)
    half_shape = jax.ShapeDtypeStruct((quarter, members, LANES), jnp.float32)
    state_shape = jax.ShapeDtypeStruct((members, rows_dev), jnp.bfloat16)
    whole2 = lambda i, *refs: (0, 0)
    whole3 = lambda i, *refs: (0, 0, 0)
    batch_of = lambda step: lambda i, order, *refs: (order[step], 0, 0)
    state_spec = pl.BlockSpec((members, rows_dev), whole2)
    half_spec = pl.BlockSpec((quarter, members, LANES), whole3)
    table_spec = pl.BlockSpec((nb, nobs), whole2)
    params = pltpu.CompilerParams(vmem_limit_bytes=48 * 1024 * 1024)
    tile_scratch = [
        pltpu.VMEM((rows_dev // LO, members, LO), jnp.bfloat16),
        pltpu.VMEM((blocks, members, LANES), jnp.float32),
    ]
    reads_specs = lambda step: [pl.BlockSpec((1, reads, nobs), batch_of(step))] * 2

    def reduce_all(keep, send):
        total = keep + lax.ppermute(send, "obs", [(j, j ^ 1) for j in range(n_obs)])
        bit = 2
        while bit < n_obs:
            total = hop(total, "obs", (bit,), n_obs)
            bit *= 2
        bit = 1
        taken = 0
        while bit < n_state:
            if HOPS[taken % len(HOPS)] == 2 and 2 * bit < n_state:
                total = hop(total, "state", (bit, 2 * bit), n_state)
                bit *= 4
            else:
                total = hop(total, "state", (bit,), n_state)
                bit *= 2
            taken += 1
        return total, lax.ppermute(total, "obs", [(j, j ^ 1) for j in range(n_obs)])

    hbm = pl.BlockSpec(memory_space=pltpu.HBM)
    keep, send, flags = pl.pallas_call(
        first_kernel,
        out_shape=(half_shape, half_shape, jax.ShapeDtypeStruct((nb * blocks,), jnp.int32)),
        in_specs=[hbm] * 4,
        out_specs=(pl.BlockSpec(memory_space=pltpu.VMEM),) * 2 + (pl.BlockSpec(memory_space=pltpu.SMEM),),
        scratch_shapes=[
            pltpu.SMEM((nb,), jnp.int32),
            pltpu.VMEM((members, rows_dev), jnp.bfloat16),
            pltpu.VMEM(obs_rows.shape, jnp.int32),
            pltpu.VMEM(obs_rows.shape, jnp.float32),
            *tile_scratch,
            pltpu.SemaphoreType.DMA((4,)),
        ],
        compiler_params=params,
        name="observe",
    )(batch_order, prior_state, obs_rows, footprint_weights)
    current = prior_state
    for step in range(nb):
        last = step == nb - 1
        own, other = reduce_all(keep, send)
        in_specs = [state_spec, half_spec, half_spec, table_spec, table_spec]
        in_specs += [pl.BlockSpec((1, members, nobs), batch_of(step))]
        args = [batch_order, lists, flags, current, own, other, obs_values, obs_errors, obs_perturbations]
        scratch = [
            pltpu.VMEM((2 * quarter, members, LANES), jnp.float32),
            pltpu.VMEM((members, rows_dev), jnp.float32),
            pltpu.SMEM((blocks + 1,), jnp.int32),
        ]
        if not last:
            in_specs += reads_specs(step + 1)
            args += [obs_rows, footprint_weights]
            scratch += tile_scratch
        outs = pl.pallas_call(
            functools.partial(step_kernel, blocks, span, step, last),
            out_shape=(state_shape,) if last else (state_shape, half_shape, half_shape),
            grid_spec=pltpu.PrefetchScalarGridSpec(
                num_scalar_prefetch=3,
                grid=(1,),
                in_specs=in_specs,
                out_specs=(state_spec,) if last else (state_spec, half_spec, half_spec),
                scratch_shapes=scratch,
            ),
            compiler_params=params,
            name="last_update" if last else "update_observe",
        )(*args)
        current = outs[0]
        if not last:
            keep, send = outs[1:]
    return current


def solution(mesh):
    return jax.shard_map(
        functools.partial(shards, mesh.shape["state"], mesh.shape["obs"]),
        mesh=mesh,
        in_specs=(P(None, ("state", "obs")), P(), P(), P(), P(), P(), P(), P()),
        out_specs=P(None, ("state", "obs")),
        check_vma=False,
    )
```

```python
import functools
import math

import jax
import jax.numpy as jnp
from jax import lax
from jax.experimental import pallas as pl
from jax.experimental.pallas import tpu as pltpu
from jax.sharding import PartitionSpec as P

OBK = 64
LANES = 128
LO = 256
GROUP = 4
HOPS = (2, 2)
HIGHEST = lax.Precision.HIGHEST
NT = (((1,), (1,)), ((), ()))
TN = (((0,), (0,)), ((), ()))


def touched_blocks(rows_ref, base, rows_dev, flags_ref):
    batches, _, nobs = rows_ref.shape
    lane = lax.broadcasted_iota(jnp.int32, (1, LANES), 1)
    bits = 16
    words = [jnp.zeros((1, 1), jnp.float32) for _ in range(batches * nobs // (OBK * bits))]
    place = 0
    for batch in range(batches):
        local = rows_ref[batch] - base
        inside = jnp.where((local >= 0) & (local < rows_dev), 1.0, 0.0)
        hits = jnp.max(inside, axis=0, keepdims=True)
        for tile in range(nobs // LANES):
            part = hits[:, tile * LANES : (tile + 1) * LANES]
            for side in (lane < OBK, lane >= OBK):
                any_hit = jnp.max(jnp.where(side, part, 0.0), axis=1, keepdims=True)
                words[place // bits] = words[place // bits] + any_hit * float(1 << (place % bits))
                place += 1
    for at, word in enumerate(words):
        packed = word[0, 0].astype(jnp.int32)
        for bit in range(bits):
            flags_ref[at * bits + bit] = (packed >> bit) & 1


def observe_into(state_ref, tiles_ref, rows_ref, weights_ref, slot, part_ref, keep_ref, send_ref, active, base, half):
    blocks = part_ref.shape[0]
    members = state_ref.shape[0]
    tiles = state_ref.shape[1] // LO
    reads = rows_ref.shape[1]
    fold = reads // 2
    for tile in range(tiles):
        tiles_ref[tile] = state_ref[:, tile * LO : (tile + 1) * LO]
    lane = lax.broadcasted_iota(jnp.int32, (fold, LANES), 1)

    def one_block(block_id, carry):
        @pl.when(active(block_id) == 0)
        def _():
            part_ref[block_id] = jnp.zeros((members, LANES), jnp.float32)

        @pl.when(active(block_id) != 0)
        def _():
            pair = block_id // 2
            odd = block_id - 2 * pair
            lanes = pl.ds(pl.multiple_of(pair * LANES, LANES), LANES)

            def folded(ref):
                top = ref[slot, :fold, lanes]
                bottom = ref[slot, fold:, lanes]
                even = jnp.where(lane < OBK, top, pltpu.roll(bottom, OBK, 1))
                other = jnp.where(lane < OBK, pltpu.roll(top, OBK, 1), bottom)
                return jnp.where(odd == 1, other, even)

            rows = folded(rows_ref) - base
            weights = folded(weights_ref)
            stacked = tiles_ref[...].reshape(tiles * members, LO)
            total = jnp.zeros((members, LANES), jnp.float32)
            for read in range(0, fold, 2):
                pick = lambda x: jnp.concatenate([x[read : read + 1], x[read + 1 : read + 2]], axis=1)
                row = pick(rows)
                weight = pick(weights)
                low = row & (LO - 1)
                high = row >> (LO.bit_length() - 1)
                chosen = (lax.broadcasted_iota(jnp.int32, (LO, LO), 0) == low).astype(jnp.float32)
                picked = jnp.dot(stacked, chosen.astype(jnp.bfloat16), preferred_element_type=jnp.float32)
                acc = jnp.zeros((members, LO), jnp.float32)
                for tile in range(tiles):
                    scale = jnp.where(high == tile, weight, 0.0)
                    acc = acc + picked[tile * members : (tile + 1) * members] * scale
                total = total + (acc[:, :LANES] + acc[:, LANES:])
            part_ref[block_id] = total + pltpu.roll(total, OBK, 1)

        return carry

    lax.fori_loop(0, blocks, one_block, 0)
    low_lane = lax.broadcasted_iota(jnp.int32, (members, LANES), 1) < OBK
    quarter = blocks // 4
    for at in range(quarter):
        for out_ref, side in ((keep_ref, half), (send_ref, 1 - half)):
            first = 2 * (side * quarter + at)
            out_ref[at] = jnp.where(low_lane, part_ref[first], part_ref[first + 1])


def block_transforms(spreads, misfits, scale):
    obs = spreads[0].shape[0]
    tiles = obs // 8
    groups = range(len(spreads))
    wide = (8, LANES)
    eye = lax.broadcasted_iota(jnp.int32, (obs, obs), 0) == lax.broadcasted_iota(jnp.int32, (obs, obs), 1)
    sublane = lax.broadcasted_iota(jnp.int32, wide, 0)
    split = lambda x: [x[i : i + 8] for i in range(0, obs, 8)]
    row = lambda x, j: jnp.broadcast_to(x[j : j + 1], (8, x.shape[1]))
    system = [
        split(eye.astype(jnp.float32) + lax.dot_general(s, s, NT, precision=HIGHEST, preferred_element_type=jnp.float32))
        for s in spreads
    ]
    right = [split(s) for s in spreads]
    left = [split(m) for m in misfits]
    scaled = [[] for _ in groups]
    for p in range(tiles):
        columns = [
            [[jnp.broadcast_to(system[g][i][:, 8 * p + j : 8 * p + j + 1], wide) for i in range(p, tiles)] for j in range(8)]
            for g in groups
        ]
        factors = [[] for _ in groups]
        inverses = [[] for _ in groups]
        for j in range(8):
            for g in groups:
                panel = columns[g]
                inverse = 1.0 / row(panel[j][0], j)
                factor = [x * inverse for x in panel[j]]
                factor[0] = jnp.where(sublane > j, factor[0], 0.0)
                for k in range(j + 1, 8):
                    pivot_row = row(panel[k][0], j)
                    panel[k] = [x - f * pivot_row for x, f in zip(panel[k], factor)]
                factors[g].append(factor)
                inverses[g].append(inverse)
        for j in range(8):
            for g in groups:
                row_s, row_r, row_l = row(system[g][p], j), row(right[g][p], j), row(left[g][p], j)
                scaled[g].append(right[g][p][j : j + 1] * inverses[g][j][j : j + 1])
                for i in range(p, tiles):
                    if i == p and j == 7:
                        continue
                    factor = factors[g][j][i - p]
                    if i > p or j < 7:
                        system[g][i] = system[g][i] - factor[:, :obs] * row_s
                    right[g][i] = right[g][i] - factor * row_r
                    left[g][i] = left[g][i] - factor * row_l
    return [
        lax.dot_general(
            jnp.concatenate(left[g], axis=0),
            jnp.concatenate(scaled[g], axis=0),
            TN,
            precision=HIGHEST,
            preferred_element_type=jnp.float32,
        )
        * (1.0 / scale)
        for g in groups
    ]


def first_kernel(
    order_hbm,
    state_hbm,
    rows_hbm,
    weights_hbm,
    keep_ref,
    send_ref,
    flags_ref,
    order_ref,
    state_ref,
    rows_ref,
    weights_ref,
    tiles_ref,
    part_ref,
    sems,
):
    pairs = ((rows_hbm, rows_ref), (order_hbm, order_ref), (state_hbm, state_ref), (weights_hbm, weights_ref))
    copies = [pltpu.make_async_copy(a, b, sems.at[i]) for i, (a, b) in enumerate(pairs)]
    for copy in copies:
        copy.start()
    blocks = part_ref.shape[0]
    rows_dev = state_ref.shape[1]
    base = lax.axis_index(("state", "obs")) * rows_dev
    half = lax.axis_index("obs") % 2
    copies[0].wait()
    touched_blocks(rows_ref, base, rows_dev, flags_ref)
    for copy in copies[1:]:
        copy.wait()
    batch = order_ref[0]
    active = lambda block_id: flags_ref[batch * blocks + block_id]
    observe_into(state_ref, tiles_ref, rows_ref, weights_ref, batch, part_ref, keep_ref, send_ref, active, base, half)


def step_kernel(
    blocks,
    span,
    step,
    last,
    order_ref,
    lists_ref,
    flags_ref,
    state_ref,
    own_ref,
    other_ref,
    values_ref,
    errors_ref,
    perturb_ref,
    *rest,
):
    if last:
        new_ref, ens_ref, acc_ref, turn_ref, named_ref = rest
    else:
        rows_ref, weights_ref, new_ref, keep_ref, send_ref, ens_ref, acc_ref, turn_ref, named_ref = rest[:9]
        tiles_ref, part_ref = rest[9:]
    members, rows_dev = state_ref.shape
    shard_id = lax.axis_index(("state", "obs"))
    half = lax.axis_index("obs") % 2
    base = shard_id * rows_dev
    batch = order_ref[step]
    quarter = blocks // 4
    scale = math.sqrt(members - 1)
    reach_rows = span * rows_dev // 2

    ens_ref[pl.ds(half * quarter, quarter)] = own_ref[...]
    ens_ref[pl.ds((1 - half) * quarter, quarter)] = other_ref[...]

    def scan(block_id, found):
        begin = (batch * blocks + block_id) * span
        look = lambda slot, hit: hit | (lists_ref[begin + slot] == shard_id).astype(jnp.int32)
        named_ref[found] = block_id
        return found + lax.fori_loop(0, span, look, jnp.int32(0))

    found = lax.fori_loop(0, blocks, scan, jnp.int32(0))

    def transposed(place):
        block_id = named_ref[place]
        pair = block_id // 2
        odd = block_id - 2 * pair
        ens = ens_ref[pair]
        lanes = pl.ds(pl.multiple_of(pair * LANES, LANES), LANES)
        mine = lax.broadcasted_iota(jnp.int32, (values_ref.shape[0], LANES), 0) == batch
        of_batch = lambda ref: jnp.sum(jnp.where(mine, ref[:, lanes], 0.0), axis=0, keepdims=True)
        error = of_batch(errors_ref)
        value = of_batch(values_ref)
        pert = perturb_ref[0, :, lanes]
        mean = jnp.sum(ens, axis=0, keepdims=True) * (1.0 / members)
        spread = (ens - mean) / (error * scale)
        misfit = (value + error * pert - ens) / error
        pad = jnp.zeros((LANES - members, LANES), jnp.float32)
        turn = lambda x: jnp.concatenate([x, pad], axis=0).T
        pick = lambda x: jnp.where(odd == 1, x[OBK:], x[:OBK])
        return pick(turn(spread)), pick(turn(misfit))

    def one_group(group, carry):
        first = group * GROUP
        for size in range(1, GROUP + 1):

            @pl.when(jnp.minimum(found - first, GROUP) == size)
            def _(size=size):
                sides = [transposed(first + slot) for slot in range(size)]
                results = block_transforms([s for s, _ in sides], [m for _, m in sides], scale)
                for slot, result in enumerate(results):
                    result = result[:members]
                    centred = result - jnp.sum(result, axis=1, keepdims=True) * (1.0 / members)
                    centred = centred[:, :members]
                    coarse = centred.astype(jnp.bfloat16)
                    fine = (centred - coarse.astype(jnp.float32)).astype(jnp.bfloat16)
                    turn_ref[first + slot] = jnp.concatenate([coarse, fine], axis=0)

        return carry

    lax.fori_loop(0, (found + GROUP - 1) // GROUP, one_group, 0)
    acc_ref[...] = state_ref[...].astype(jnp.float32)

    def update(place, carry):
        centre = lists_ref[(batch * blocks + named_ref[place]) * span] * rows_dev + rows_dev // 2
        both = turn_ref[place]
        for start in range(0, rows_dev, LO):
            cols = slice(start, start + LO)
            product = jnp.dot(both, state_ref[:, cols], preferred_element_type=jnp.float32)
            positions = base + start + lax.broadcasted_iota(jnp.int32, (1, LO), 1)
            distance = jnp.abs(positions - centre).astype(jnp.float32) / reach_rows
            hat = jnp.maximum(0.0, 1.0 - distance)
            acc_ref[:, cols] += (product[:members] + product[members:]) * (hat * hat)
        return carry

    lax.fori_loop(0, found, update, 0)
    new_ref[...] = acc_ref[...].astype(jnp.bfloat16)
    if not last:
        following = order_ref[step + 1] * blocks
        active = lambda block_id: flags_ref[following + block_id]
        observe_into(new_ref, tiles_ref, rows_ref, weights_ref, 0, part_ref, keep_ref, send_ref, active, base, half)


def hop(x, axis, flips, size):
    send = lambda bits: lax.ppermute(x, axis, [(j, j ^ bits) for j in range(size)])
    if len(flips) == 1:
        return x + send(flips[0])
    one, two = flips
    a, b, c = send(one), send(two), send(one | two)
    return (x + a) + (b + c)


def shards(
    n_state,
    n_obs,
    prior_state,
    batch_order,
    obs_rows,
    footprint_weights,
    obs_values,
    obs_errors,
    obs_perturbations,
    target_lists,
):
    members, rows_dev = prior_state.shape
    nb, blocks, span = target_lists.shape
    reads, nobs = obs_rows.shape[1:]
    quarter = blocks // 4
    lists = target_lists.reshape(-1)
    half_shape = jax.ShapeDtypeStruct((quarter, members, LANES), jnp.float32)
    state_shape = jax.ShapeDtypeStruct((members, rows_dev), jnp.bfloat16)
    whole2 = lambda i, *refs: (0, 0)
    whole3 = lambda i, *refs: (0, 0, 0)
    batch_of = lambda step: lambda i, order, *refs: (order[step], 0, 0)
    state_spec = pl.BlockSpec((members, rows_dev), whole2)
    half_spec = pl.BlockSpec((quarter, members, LANES), whole3)
    table_spec = pl.BlockSpec((nb, nobs), whole2)
    params = pltpu.CompilerParams(vmem_limit_bytes=48 * 1024 * 1024)
    tile_scratch = [
        pltpu.VMEM((rows_dev // LO, members, LO), jnp.bfloat16),
        pltpu.VMEM((blocks, members, LANES), jnp.float32),
    ]
    reads_specs = lambda step: [pl.BlockSpec((1, reads, nobs), batch_of(step))] * 2

    def reduce_all(keep, send):
        total = keep + lax.ppermute(send, "obs", [(j, j ^ 1) for j in range(n_obs)])
        bit = 2
        while bit < n_obs:
            total = hop(total, "obs", (bit,), n_obs)
            bit *= 2
        bit = 1
        taken = 0
        while bit < n_state:
            if HOPS[taken % len(HOPS)] == 2 and 2 * bit < n_state:
                total = hop(total, "state", (bit, 2 * bit), n_state)
                bit *= 4
            else:
                total = hop(total, "state", (bit,), n_state)
                bit *= 2
            taken += 1
        return total, lax.ppermute(total, "obs", [(j, j ^ 1) for j in range(n_obs)])

    hbm = pl.BlockSpec(memory_space=pltpu.HBM)
    keep, send, flags = pl.pallas_call(
        first_kernel,
        out_shape=(half_shape, half_shape, jax.ShapeDtypeStruct((nb * blocks,), jnp.int32)),
        in_specs=[hbm] * 4,
        out_specs=(pl.BlockSpec(memory_space=pltpu.VMEM),) * 2 + (pl.BlockSpec(memory_space=pltpu.SMEM),),
        scratch_shapes=[
            pltpu.SMEM((nb,), jnp.int32),
            pltpu.VMEM((members, rows_dev), jnp.bfloat16),
            pltpu.VMEM(obs_rows.shape, jnp.int32),
            pltpu.VMEM(obs_rows.shape, jnp.float32),
            *tile_scratch,
            pltpu.SemaphoreType.DMA((4,)),
        ],
        compiler_params=pltpu.CompilerParams(vmem_limit_bytes=62500000),
        name="observe",
    )(batch_order, prior_state, obs_rows, footprint_weights)
    current = prior_state
    for step in range(nb):
        last = step == nb - 1
        own, other = reduce_all(keep, send)
        in_specs = [state_spec, half_spec, half_spec, table_spec, table_spec]
        in_specs += [pl.BlockSpec((1, members, nobs), batch_of(step))]
        args = [batch_order, lists, flags, current, own, other, obs_values, obs_errors, obs_perturbations]
        scratch = [
            pltpu.VMEM((2 * quarter, members, LANES), jnp.float32),
            pltpu.VMEM((members, rows_dev), jnp.float32),
            pltpu.VMEM((blocks, 2 * members, members), jnp.bfloat16),
            pltpu.SMEM((blocks + 1,), jnp.int32),
        ]
        if not last:
            in_specs += reads_specs(step + 1)
            args += [obs_rows, footprint_weights]
            scratch += tile_scratch
        outs = pl.pallas_call(
            functools.partial(step_kernel, blocks, span, step, last),
            out_shape=(state_shape,) if last else (state_shape, half_shape, half_shape),
            grid_spec=pltpu.PrefetchScalarGridSpec(
                num_scalar_prefetch=3,
                grid=(1,),
                in_specs=in_specs,
                out_specs=(state_spec,) if last else (state_spec, half_spec, half_spec),
                scratch_shapes=scratch,
            ),
            compiler_params=params,
            name="last_update" if last else "update_observe",
        )(*args)
        current = outs[0]
        if not last:
            keep, send = outs[1:]
    return current


def solution(mesh):
    return jax.shard_map(
        functools.partial(shards, mesh.shape["state"], mesh.shape["obs"]),
        mesh=mesh,
        in_specs=(P(None, ("state", "obs")), P(), P(), P(), P(), P(), P(), P()),
        out_specs=P(None, ("state", "obs")),
        check_vma=False,
    )
```

```python
import functools
import math

import jax
import jax.numpy as jnp
from jax import lax
from jax.experimental import pallas as pl
from jax.experimental.pallas import tpu as pltpu
from jax.sharding import PartitionSpec as P

OBK = 64
LANES = 128
LO = 256
GROUP = 4
HOPS = (2, 2)
HIGHEST = lax.Precision.HIGHEST
NT = (((1,), (1,)), ((), ()))
TN = (((0,), (0,)), ((), ()))


def touched_blocks(rows_ref, base, rows_dev, flags_ref):
    batches, reads, nobs = rows_ref.shape
    fold = reads // 2
    lane = lax.broadcasted_iota(jnp.int32, (1, LANES), 1)
    read = lax.broadcasted_iota(jnp.int32, (reads, nobs), 0)
    last_pass = jnp.where(read < fold, read, read - fold) >= fold - 2
    bits = 16
    words = [jnp.zeros((1, 1), jnp.float32) for _ in range(2 * batches * nobs // (OBK * bits))]
    place = 0
    for batch in range(batches):
        local = rows_ref[batch] - base
        inside = jnp.where((local >= 0) & (local < rows_dev), 1.0, 0.0)
        for part in (jnp.where(last_pass, 0.0, inside), jnp.where(last_pass, inside, 0.0)):
            hits = jnp.max(part, axis=0, keepdims=True)
            for tile in range(nobs // LANES):
                some = hits[:, tile * LANES : (tile + 1) * LANES]
                for side in (lane < OBK, lane >= OBK):
                    any_hit = jnp.max(jnp.where(side, some, 0.0), axis=1, keepdims=True)
                    words[place // bits] = words[place // bits] + any_hit * float(1 << (place % bits))
                    place += 1
    for at, word in enumerate(words):
        packed = word[0, 0].astype(jnp.int32)
        for bit in range(bits):
            flags_ref[at * bits + bit] = (packed >> bit) & 1


def observe_into(state_ref, tiles_ref, rows_ref, weights_ref, slot, part_ref, keep_ref, send_ref, active, base, half):
    blocks = part_ref.shape[0]
    members = state_ref.shape[0]
    tiles = state_ref.shape[1] // LO
    reads = rows_ref.shape[1]
    fold = reads // 2
    for tile in range(tiles):
        tiles_ref[tile] = state_ref[:, tile * LO : (tile + 1) * LO]
    lane = lax.broadcasted_iota(jnp.int32, (fold, LANES), 1)

    def one_pass(block_id, starts):
        pair = block_id // 2
        odd = block_id - 2 * pair
        lanes = pl.ds(pl.multiple_of(pair * LANES, LANES), LANES)

        def folded(ref):
            top = ref[slot, :fold, lanes]
            bottom = ref[slot, fold:, lanes]
            even = jnp.where(lane < OBK, top, pltpu.roll(bottom, OBK, 1))
            other = jnp.where(lane < OBK, pltpu.roll(top, OBK, 1), bottom)
            return jnp.where(odd == 1, other, even)

        rows = folded(rows_ref) - base
        weights = folded(weights_ref)
        stacked = tiles_ref[...].reshape(tiles * members, LO)
        total = jnp.zeros((members, LANES), jnp.float32)
        for read in starts:
            pick = lambda x: jnp.concatenate([x[read : read + 1], x[read + 1 : read + 2]], axis=1)
            row = pick(rows)
            weight = pick(weights)
            low = row & (LO - 1)
            high = row >> (LO.bit_length() - 1)
            chosen = (lax.broadcasted_iota(jnp.int32, (LO, LO), 0) == low).astype(jnp.float32)
            picked = jnp.dot(stacked, chosen.astype(jnp.bfloat16), preferred_element_type=jnp.float32)
            acc = jnp.zeros((members, LO), jnp.float32)
            for tile in range(tiles):
                scale = jnp.where(high == tile, weight, 0.0)
                acc = acc + picked[tile * members : (tile + 1) * members] * scale
            total = total + (acc[:, :LANES] + acc[:, LANES:])
        part_ref[block_id] += total + pltpu.roll(total, OBK, 1)

    def one_block(block_id, carry):
        part_ref[block_id] = jnp.zeros((members, LANES), jnp.float32)
        for part, starts in enumerate((range(0, fold - 2, 2), (fold - 2,))):
            pl.when(active(block_id, part) != 0)(functools.partial(one_pass, block_id, starts))
        return carry

    lax.fori_loop(0, blocks, one_block, 0)
    low_lane = lax.broadcasted_iota(jnp.int32, (members, LANES), 1) < OBK
    quarter = blocks // 4
    for at in range(quarter):
        for out_ref, side in ((keep_ref, half), (send_ref, 1 - half)):
            first = 2 * (side * quarter + at)
            out_ref[at] = jnp.where(low_lane, part_ref[first], part_ref[first + 1])


def in_two(x):
    coarse = x.astype(jnp.bfloat16)
    return coarse, (x - coarse.astype(jnp.float32)).astype(jnp.bfloat16)


def block_transforms(spreads, misfits, scale):
    obs = spreads[0].shape[0]
    tiles = obs // 8
    groups = range(len(spreads))
    wide = (8, LANES)
    eye = lax.broadcasted_iota(jnp.int32, (obs, obs), 0) == lax.broadcasted_iota(jnp.int32, (obs, obs), 1)
    sublane = lax.broadcasted_iota(jnp.int32, wide, 0)
    split = lambda x: [x[i : i + 8] for i in range(0, obs, 8)]
    row = lambda x, j: jnp.broadcast_to(x[j : j + 1], (8, x.shape[1]))
    system = [
        split(eye.astype(jnp.float32) + lax.dot_general(s, s, NT, precision=HIGHEST, preferred_element_type=jnp.float32))
        for s in spreads
    ]
    right = [split(s) for s in spreads]
    left = [split(m) for m in misfits]
    scaled = [[] for _ in groups]
    for p in range(tiles):
        columns = [
            [[jnp.broadcast_to(system[g][i][:, 8 * p + j : 8 * p + j + 1], wide) for i in range(p, tiles)] for j in range(8)]
            for g in groups
        ]
        factors = [[] for _ in groups]
        inverses = [[] for _ in groups]
        for j in range(8):
            for g in groups:
                panel = columns[g]
                inverse = 1.0 / row(panel[j][0], j)
                factor = [x * inverse for x in panel[j]]
                factor[0] = jnp.where(sublane > j, factor[0], 0.0)
                for k in range(j + 1, 8):
                    pivot_row = row(panel[k][0], j)
                    panel[k] = [x - f * pivot_row for x, f in zip(panel[k], factor)]
                factors[g].append(factor)
                inverses[g].append(inverse)
        for j in range(8):
            for g in groups:
                row_s, row_r, row_l = row(system[g][p], j), row(right[g][p], j), row(left[g][p], j)
                scaled[g].append(right[g][p][j : j + 1] * inverses[g][j][j : j + 1])
                for i in range(p, tiles):
                    if i == p and j == 7:
                        continue
                    factor = factors[g][j][i - p]
                    if i > p or j < 7:
                        system[g][i] = system[g][i] - factor[:, :obs] * row_s
                    right[g][i] = right[g][i] - factor * row_r
                    left[g][i] = left[g][i] - factor * row_l
    results = []
    for g in groups:
        coarse_l, fine_l = in_two(jnp.concatenate(left[g], axis=0))
        coarse_r, fine_r = in_two(jnp.concatenate(scaled[g], axis=0))
        product = lax.dot_general(
            jnp.concatenate([coarse_l, coarse_l, fine_l], axis=0),
            jnp.concatenate([coarse_r, fine_r, coarse_r], axis=0),
            TN,
            preferred_element_type=jnp.float32,
        )
        results.append(product * (1.0 / scale))
    return results


def first_kernel(
    order_hbm,
    state_hbm,
    rows_hbm,
    weights_hbm,
    keep_ref,
    send_ref,
    flags_ref,
    order_ref,
    state_ref,
    rows_ref,
    weights_ref,
    tiles_ref,
    part_ref,
    sems,
):
    pairs = ((rows_hbm, rows_ref), (order_hbm, order_ref), (state_hbm, state_ref), (weights_hbm, weights_ref))
    copies = [pltpu.make_async_copy(a, b, sems.at[i]) for i, (a, b) in enumerate(pairs)]
    for copy in copies:
        copy.start()
    blocks = part_ref.shape[0]
    rows_dev = state_ref.shape[1]
    base = lax.axis_index(("state", "obs")) * rows_dev
    half = lax.axis_index("obs") % 2
    copies[0].wait()
    touched_blocks(rows_ref, base, rows_dev, flags_ref)
    for copy in copies[1:]:
        copy.wait()
    batch = order_ref[0]
    active = lambda block_id, part: flags_ref[(2 * batch + part) * blocks + block_id]
    observe_into(state_ref, tiles_ref, rows_ref, weights_ref, batch, part_ref, keep_ref, send_ref, active, base, half)


def step_kernel(
    blocks,
    span,
    step,
    last,
    order_ref,
    lists_ref,
    flags_ref,
    state_ref,
    own_ref,
    other_ref,
    values_ref,
    errors_ref,
    perturb_ref,
    *rest,
):
    if last:
        new_ref, ens_ref, acc_ref, turn_ref, named_ref = rest
    else:
        rows_ref, weights_ref, new_ref, keep_ref, send_ref, ens_ref, acc_ref, turn_ref, named_ref = rest[:9]
        tiles_ref, part_ref = rest[9:]
    members, rows_dev = state_ref.shape
    shard_id = lax.axis_index(("state", "obs"))
    half = lax.axis_index("obs") % 2
    base = shard_id * rows_dev
    batch = order_ref[step]
    quarter = blocks // 4
    scale = math.sqrt(members - 1)
    reach_rows = span * rows_dev // 2

    ens_ref[pl.ds(half * quarter, quarter)] = own_ref[...]
    ens_ref[pl.ds((1 - half) * quarter, quarter)] = other_ref[...]

    def scan(block_id, found):
        begin = (batch * blocks + block_id) * span
        look = lambda slot, hit: hit | (lists_ref[begin + slot] == shard_id).astype(jnp.int32)
        named_ref[found] = block_id
        return found + lax.fori_loop(0, span, look, jnp.int32(0))

    found = lax.fori_loop(0, blocks, scan, jnp.int32(0))

    def transposed(place):
        block_id = named_ref[place]
        pair = block_id // 2
        odd = block_id - 2 * pair
        ens = ens_ref[pair]
        lanes = pl.ds(pl.multiple_of(pair * LANES, LANES), LANES)
        mine = lax.broadcasted_iota(jnp.int32, (values_ref.shape[0], LANES), 0) == batch
        of_batch = lambda ref: jnp.sum(jnp.where(mine, ref[:, lanes], 0.0), axis=0, keepdims=True)
        error = of_batch(errors_ref)
        value = of_batch(values_ref)
        pert = perturb_ref[0, :, lanes]
        mean = jnp.sum(ens, axis=0, keepdims=True) * (1.0 / members)
        spread = (ens - mean) * (1.0 / (error * scale))
        misfit = (value + error * pert - ens) * (1.0 / error)
        pad = jnp.zeros((LANES - members, LANES), jnp.float32)
        turn = lambda x: jnp.concatenate([x, pad], axis=0).T
        pick = lambda x: jnp.where(odd == 1, x[OBK:], x[:OBK])
        return pick(turn(spread)), pick(turn(misfit))

    def one_group(group, carry):
        first = group * GROUP
        for size in range(1, GROUP + 1):

            @pl.when(jnp.minimum(found - first, GROUP) == size)
            def _(size=size):
                sides = [transposed(first + slot) for slot in range(size)]
                results = block_transforms([s for s, _ in sides], [m for _, m in sides], scale)
                for slot, result in enumerate(results):
                    result = result[:members]
                    centred = result - jnp.sum(result, axis=1, keepdims=True) * (1.0 / members)
                    centred = centred[:, :members]
                    turn_ref[first + slot] = jnp.concatenate(in_two(centred), axis=0)

        return carry

    lax.fori_loop(0, (found + GROUP - 1) // GROUP, one_group, 0)
    acc_ref[...] = state_ref[...].astype(jnp.float32)

    def update(place, carry):
        centre = lists_ref[(batch * blocks + named_ref[place]) * span] * rows_dev + rows_dev // 2
        both = turn_ref[place]
        for start in range(0, rows_dev, LO):
            cols = slice(start, start + LO)
            product = jnp.dot(both, state_ref[:, cols], preferred_element_type=jnp.float32)
            positions = base + start + lax.broadcasted_iota(jnp.int32, (1, LO), 1)
            distance = jnp.abs(positions - centre).astype(jnp.float32) / reach_rows
            hat = jnp.maximum(0.0, 1.0 - distance)
            acc_ref[:, cols] += (product[:members] + product[members:]) * (hat * hat)
        return carry

    lax.fori_loop(0, found, update, 0)
    new_ref[...] = acc_ref[...].astype(jnp.bfloat16)
    if not last:
        following = order_ref[step + 1]
        active = lambda block_id, part: flags_ref[(2 * following + part) * blocks + block_id]
        observe_into(new_ref, tiles_ref, rows_ref, weights_ref, 0, part_ref, keep_ref, send_ref, active, base, half)


def hop(x, axis, flips, size):
    send = lambda bits: lax.ppermute(x, axis, [(j, j ^ bits) for j in range(size)])
    if len(flips) == 1:
        return x + send(flips[0])
    one, two = flips
    a, b, c = send(one), send(two), send(one | two)
    return (x + a) + (b + c)


def shards(
    n_state,
    n_obs,
    prior_state,
    batch_order,
    obs_rows,
    footprint_weights,
    obs_values,
    obs_errors,
    obs_perturbations,
    target_lists,
):
    members, rows_dev = prior_state.shape
    nb, blocks, span = target_lists.shape
    reads, nobs = obs_rows.shape[1:]
    quarter = blocks // 4
    lists = target_lists.reshape(-1)
    half_shape = jax.ShapeDtypeStruct((quarter, members, LANES), jnp.float32)
    state_shape = jax.ShapeDtypeStruct((members, rows_dev), jnp.bfloat16)
    whole2 = lambda i, *refs: (0, 0)
    whole3 = lambda i, *refs: (0, 0, 0)
    batch_of = lambda step: lambda i, order, *refs: (order[step], 0, 0)
    state_spec = pl.BlockSpec((members, rows_dev), whole2)
    half_spec = pl.BlockSpec((quarter, members, LANES), whole3)
    table_spec = pl.BlockSpec((nb, nobs), whole2)
    params = pltpu.CompilerParams(vmem_limit_bytes=48 * 1024 * 1024)
    tile_scratch = [
        pltpu.VMEM((rows_dev // LO, members, LO), jnp.bfloat16),
        pltpu.VMEM((blocks, members, LANES), jnp.float32),
    ]
    reads_specs = lambda step: [pl.BlockSpec((1, reads, nobs), batch_of(step))] * 2

    def reduce_all(keep, send):
        total = keep + lax.ppermute(send, "obs", [(j, j ^ 1) for j in range(n_obs)])
        bit = 2
        while bit < n_obs:
            total = hop(total, "obs", (bit,), n_obs)
            bit *= 2
        bit = 1
        taken = 0
        while bit < n_state:
            if HOPS[taken % len(HOPS)] == 2 and 2 * bit < n_state:
                total = hop(total, "state", (bit, 2 * bit), n_state)
                bit *= 4
            else:
                total = hop(total, "state", (bit,), n_state)
                bit *= 2
            taken += 1
        return total, lax.ppermute(total, "obs", [(j, j ^ 1) for j in range(n_obs)])

    hbm = pl.BlockSpec(memory_space=pltpu.HBM)
    keep, send, flags = pl.pallas_call(
        first_kernel,
        out_shape=(half_shape, half_shape, jax.ShapeDtypeStruct((2 * nb * blocks,), jnp.int32)),
        in_specs=[hbm] * 4,
        out_specs=(pl.BlockSpec(memory_space=pltpu.VMEM),) * 2 + (pl.BlockSpec(memory_space=pltpu.SMEM),),
        scratch_shapes=[
            pltpu.SMEM((nb,), jnp.int32),
            pltpu.VMEM((members, rows_dev), jnp.bfloat16),
            pltpu.VMEM(obs_rows.shape, jnp.int32),
            pltpu.VMEM(obs_rows.shape, jnp.float32),
            *tile_scratch,
            pltpu.SemaphoreType.DMA((4,)),
        ],
        compiler_params=pltpu.CompilerParams(vmem_limit_bytes=62500000),
        name="observe",
    )(batch_order, prior_state, obs_rows, footprint_weights)
    current = prior_state
    for step in range(nb):
        last = step == nb - 1
        own, other = reduce_all(keep, send)
        in_specs = [state_spec, half_spec, half_spec, table_spec, table_spec]
        in_specs += [pl.BlockSpec((1, members, nobs), batch_of(step))]
        args = [batch_order, lists, flags, current, own, other, obs_values, obs_errors, obs_perturbations]
        scratch = [
            pltpu.VMEM((2 * quarter, members, LANES), jnp.float32),
            pltpu.VMEM((members, rows_dev), jnp.float32),
            pltpu.VMEM((blocks, 2 * members, members), jnp.bfloat16),
            pltpu.SMEM((blocks + 1,), jnp.int32),
        ]
        if not last:
            in_specs += reads_specs(step + 1)
            args += [obs_rows, footprint_weights]
            scratch += tile_scratch
        outs = pl.pallas_call(
            functools.partial(step_kernel, blocks, span, step, last),
            out_shape=(state_shape,) if last else (state_shape, half_shape, half_shape),
            grid_spec=pltpu.PrefetchScalarGridSpec(
                num_scalar_prefetch=3,
                grid=(1,),
                in_specs=in_specs,
                out_specs=(state_spec,) if last else (state_spec, half_spec, half_spec),
                scratch_shapes=scratch,
            ),
            compiler_params=params,
            name="last_update" if last else "update_observe",
        )(*args)
        current = outs[0]
        if not last:
            keep, send = outs[1:]
    return current


def solution(mesh):
    return jax.shard_map(
        functools.partial(shards, mesh.shape["state"], mesh.shape["obs"]),
        mesh=mesh,
        in_specs=(P(None, ("state", "obs")), P(), P(), P(), P(), P(), P(), P()),
        out_specs=P(None, ("state", "obs")),
        check_vma=False,
    )
```

```python
import functools
import math

import jax
import jax.numpy as jnp
from jax import lax
from jax.experimental import pallas as pl
from jax.experimental.pallas import tpu as pltpu
from jax.sharding import PartitionSpec as P

OBK = 64
LANES = 128
LO = 256
GROUP = 4
HOPS = (2, 2)
HIGHEST = lax.Precision.HIGHEST
NT = (((1,), (1,)), ((), ()))
TN = (((0,), (0,)), ((), ()))


def touched_blocks(rows_ref, base, rows_dev, flags_ref):
    batches, reads, nobs = rows_ref.shape
    fold = reads // 2
    lane = lax.broadcasted_iota(jnp.int32, (1, LANES), 1)
    read = lax.broadcasted_iota(jnp.int32, (reads, nobs), 0)
    last_pass = jnp.where(read < fold, read, read - fold) >= fold - 2
    bits = 16
    words = [jnp.zeros((1, 1), jnp.float32) for _ in range(2 * batches * nobs // (OBK * bits))]
    place = 0
    for batch in range(batches):
        local = rows_ref[batch] - base
        inside = jnp.where((local >= 0) & (local < rows_dev), 1.0, 0.0)
        for part in (jnp.where(last_pass, 0.0, inside), jnp.where(last_pass, inside, 0.0)):
            hits = jnp.max(part, axis=0, keepdims=True)
            for tile in range(nobs // LANES):
                some = hits[:, tile * LANES : (tile + 1) * LANES]
                for side in (lane < OBK, lane >= OBK):
                    any_hit = jnp.max(jnp.where(side, some, 0.0), axis=1, keepdims=True)
                    words[place // bits] = words[place // bits] + any_hit * float(1 << (place % bits))
                    place += 1
    for at, word in enumerate(words):
        packed = word[0, 0].astype(jnp.int32)
        for bit in range(bits):
            flags_ref[at * bits + bit] = (packed >> bit) & 1


def observe_into(state_ref, tiles_ref, rows_ref, weights_ref, slot, part_ref, keep_ref, send_ref, active, base, half):
    blocks = part_ref.shape[0]
    members = state_ref.shape[0]
    tiles = state_ref.shape[1] // LO
    reads = rows_ref.shape[1]
    fold = reads // 2
    for tile in range(tiles):
        tiles_ref[tile] = state_ref[:, tile * LO : (tile + 1) * LO]
    lane = lax.broadcasted_iota(jnp.int32, (fold, LANES), 1)

    def one_pass(block_id, starts):
        pair = block_id // 2
        odd = block_id - 2 * pair
        lanes = pl.ds(pl.multiple_of(pair * LANES, LANES), LANES)

        def folded(ref):
            top = ref[slot, :fold, lanes]
            bottom = ref[slot, fold:, lanes]
            even = jnp.where(lane < OBK, top, pltpu.roll(bottom, OBK, 1))
            other = jnp.where(lane < OBK, pltpu.roll(top, OBK, 1), bottom)
            return jnp.where(odd == 1, other, even)

        rows = folded(rows_ref) - base
        weights = folded(weights_ref)
        stacked = tiles_ref[...].reshape(tiles * members, LO)
        total = jnp.zeros((members, LANES), jnp.float32)
        for read in starts:
            pick = lambda x: jnp.concatenate([x[read : read + 1], x[read + 1 : read + 2]], axis=1)
            row = pick(rows)
            weight = pick(weights)
            low = row & (LO - 1)
            high = row >> (LO.bit_length() - 1)
            chosen = (lax.broadcasted_iota(jnp.int32, (LO, LO), 0) == low).astype(jnp.float32)
            picked = jnp.dot(stacked, chosen.astype(jnp.bfloat16), preferred_element_type=jnp.float32)
            acc = jnp.zeros((members, LO), jnp.float32)
            for tile in range(tiles):
                scale = jnp.where(high == tile, weight, 0.0)
                acc = acc + picked[tile * members : (tile + 1) * members] * scale
            total = total + (acc[:, :LANES] + acc[:, LANES:])
        part_ref[block_id] += total + pltpu.roll(total, OBK, 1)

    def one_block(block_id, carry):
        part_ref[block_id] = jnp.zeros((members, LANES), jnp.float32)
        for part, starts in enumerate((range(0, fold - 2, 2), (fold - 2,))):
            pl.when(active(block_id, part) != 0)(functools.partial(one_pass, block_id, starts))
        return carry

    lax.fori_loop(0, blocks, one_block, 0)
    low_lane = lax.broadcasted_iota(jnp.int32, (members, LANES), 1) < OBK
    quarter = blocks // 4
    for at in range(quarter):
        for out_ref, side in ((keep_ref, half), (send_ref, 1 - half)):
            first = 2 * (side * quarter + at)
            out_ref[at] = jnp.where(low_lane, part_ref[first], part_ref[first + 1])


def in_two(x):
    coarse = x.astype(jnp.bfloat16)
    return coarse, (x - coarse.astype(jnp.float32)).astype(jnp.bfloat16)


def block_transforms(spreads, misfits, scale):
    obs = spreads[0].shape[0]
    tiles = obs // 8
    groups = range(len(spreads))
    wide = (8, LANES)
    eye = lax.broadcasted_iota(jnp.int32, (obs, obs), 0) == lax.broadcasted_iota(jnp.int32, (obs, obs), 1)
    sublane = lax.broadcasted_iota(jnp.int32, wide, 0)
    split = lambda x: [x[i : i + 8] for i in range(0, obs, 8)]
    row = lambda x, j: jnp.broadcast_to(x[j : j + 1], (8, x.shape[1]))
    system = [
        split(eye.astype(jnp.float32) + lax.dot_general(s, s, NT, precision=HIGHEST, preferred_element_type=jnp.float32))
        for s in spreads
    ]
    right = [split(s) for s in spreads]
    left = [split(m) for m in misfits]
    scaled = [[] for _ in groups]
    for p in range(tiles):
        columns = [
            [[jnp.broadcast_to(system[g][i][:, 8 * p + j : 8 * p + j + 1], wide) for i in range(p, tiles)] for j in range(8)]
            for g in groups
        ]
        factors = [[] for _ in groups]
        inverses = [[] for _ in groups]
        for j in range(8):
            for g in groups:
                panel = columns[g]
                inverse = 1.0 / row(panel[j][0], j)
                factor = [x * inverse for x in panel[j]]
                factor[0] = jnp.where(sublane > j, factor[0], 0.0)
                for k in range(j + 1, 8):
                    pivot_row = row(panel[k][0], j)
                    panel[k] = [x - f * pivot_row for x, f in zip(panel[k], factor)]
                factors[g].append(factor)
                inverses[g].append(inverse)
        for j in range(8):
            for g in groups:
                row_s, row_r, row_l = row(system[g][p], j), row(right[g][p], j), row(left[g][p], j)
                scaled[g].append(right[g][p][j : j + 1] * inverses[g][j][j : j + 1])
                for i in range(p, tiles):
                    if i == p and j == 7:
                        continue
                    factor = factors[g][j][i - p]
                    if i > p or j < 7:
                        system[g][i] = system[g][i] - factor[:, :obs] * row_s
                    right[g][i] = right[g][i] - factor * row_r
                    left[g][i] = left[g][i] - factor * row_l
    results = []
    for g in groups:
        coarse_l, fine_l = in_two(jnp.concatenate(left[g], axis=0))
        coarse_r, fine_r = in_two(jnp.concatenate(scaled[g], axis=0))
        product = lax.dot_general(
            jnp.concatenate([coarse_l, coarse_l, fine_l], axis=0),
            jnp.concatenate([coarse_r, fine_r, coarse_r], axis=0),
            TN,
            preferred_element_type=jnp.float32,
        )
        results.append(product * (1.0 / scale))
    return results


def first_kernel(
    order_hbm,
    state_hbm,
    rows_hbm,
    weights_hbm,
    keep_ref,
    send_ref,
    flags_ref,
    order_ref,
    state_ref,
    rows_ref,
    weights_ref,
    tiles_ref,
    part_ref,
    sems,
):
    pairs = ((rows_hbm, rows_ref), (order_hbm, order_ref), (state_hbm, state_ref), (weights_hbm, weights_ref))
    copies = [pltpu.make_async_copy(a, b, sems.at[i]) for i, (a, b) in enumerate(pairs)]
    for copy in copies:
        copy.start()
    blocks = part_ref.shape[0]
    rows_dev = state_ref.shape[1]
    base = lax.axis_index(("state", "obs")) * rows_dev
    half = lax.axis_index("obs") % 2
    copies[0].wait()
    touched_blocks(rows_ref, base, rows_dev, flags_ref)
    for copy in copies[1:]:
        copy.wait()
    batch = order_ref[0]
    active = lambda block_id, part: flags_ref[(2 * batch + part) * blocks + block_id]
    observe_into(state_ref, tiles_ref, rows_ref, weights_ref, batch, part_ref, keep_ref, send_ref, active, base, half)


def step_kernel(
    blocks,
    span,
    step,
    last,
    order_ref,
    lists_ref,
    flags_ref,
    state_ref,
    own_ref,
    other_ref,
    values_ref,
    errors_ref,
    perturb_ref,
    *rest,
):
    if last:
        new_ref, ens_ref, acc_ref, turn_ref, named_ref = rest
    else:
        rows_ref, weights_ref, new_ref, keep_ref, send_ref, ens_ref, acc_ref, turn_ref, named_ref = rest[:9]
        tiles_ref, part_ref = rest[9:]
    members, rows_dev = state_ref.shape
    shard_id = lax.axis_index(("state", "obs"))
    half = lax.axis_index("obs") % 2
    base = shard_id * rows_dev
    batch = order_ref[step]
    quarter = blocks // 4
    scale = math.sqrt(members - 1)
    reach_rows = span * rows_dev // 2

    ens_ref[pl.ds(half * quarter, quarter)] = own_ref[...]
    ens_ref[pl.ds((1 - half) * quarter, quarter)] = other_ref[...]

    def scan(block_id, found):
        begin = (batch * blocks + block_id) * span
        look = lambda slot, hit: hit | (lists_ref[begin + slot] == shard_id).astype(jnp.int32)
        named_ref[found] = block_id
        return found + lax.fori_loop(0, span, look, jnp.int32(0))

    found = lax.fori_loop(0, blocks, scan, jnp.int32(0))

    def transposed(place):
        block_id = named_ref[place]
        pair = block_id // 2
        odd = block_id - 2 * pair
        ens = ens_ref[pair]
        lanes = pl.ds(pl.multiple_of(pair * LANES, LANES), LANES)
        mine = lax.broadcasted_iota(jnp.int32, (values_ref.shape[0], LANES), 0) == batch
        of_batch = lambda ref: jnp.sum(jnp.where(mine, ref[:, lanes], 0.0), axis=0, keepdims=True)
        error = of_batch(errors_ref)
        value = of_batch(values_ref)
        pert = perturb_ref[0, :, lanes]
        mean = jnp.sum(ens, axis=0, keepdims=True) * (1.0 / members)
        spread = (ens - mean) * (1.0 / (error * scale))
        misfit = (value + error * pert - ens) * (1.0 / error)
        pad = jnp.zeros((LANES - members, LANES), jnp.float32)
        turn = lambda x: jnp.concatenate([x, pad], axis=0).T
        pick = lambda x: jnp.where(odd == 1, x[OBK:], x[:OBK])
        return pick(turn(spread)), pick(turn(misfit))

    tiles = rows_dev // LO
    turn_ref[...] = jnp.zeros(turn_ref.shape, jnp.bfloat16)
    acc_ref[...] = state_ref[...].astype(jnp.float32)

    def one_group(group, carry):
        first = group * GROUP
        for size in range(1, GROUP + 1):

            @pl.when(jnp.minimum(found - first, GROUP) == size)
            def _(size=size):
                sides = [transposed(first + slot) for slot in range(size)]
                results = block_transforms([s for s, _ in sides], [m for _, m in sides], scale)
                blank = jnp.zeros((members, LANES), jnp.float32)
                for slot, result in enumerate(results):
                    result = result[:members]
                    centred = result - jnp.sum(result, axis=1, keepdims=True) * (1.0 / members)
                    centred = jnp.where(lax.broadcasted_iota(jnp.int32, centred.shape, 1) < members, centred, 0.0)
                    coarse, fine = (x.astype(jnp.float32) for x in in_two(centred))
                    beside = pltpu.roll(jnp.concatenate([fine, blank], axis=1), members, 1)
                    beside = beside + jnp.concatenate([coarse, blank], axis=1)
                    turn_ref[slot * members : (slot + 1) * members] = beside.astype(jnp.bfloat16)

        centres, valid = [], []
        for slot in range(GROUP):
            place = jnp.minimum(first + slot, found - 1)
            centres.append(lists_ref[(batch * blocks + named_ref[place]) * span] * rows_dev + rows_dev // 2)
            valid.append((first + slot < found).astype(jnp.float32))
        for tile in range(tiles):
            cols = slice(tile * LO, (tile + 1) * LO)
            twice = jnp.concatenate([state_ref[:, cols]] * 2, axis=0)
            product = jnp.dot(turn_ref[:, : 2 * members], twice, preferred_element_type=jnp.float32)
            value = acc_ref[:, cols]
            positions = base + tile * LO + lax.broadcasted_iota(jnp.int32, (1, LO), 1)
            for slot in range(GROUP):
                distance = jnp.abs(positions - centres[slot]).astype(jnp.float32) / reach_rows
                hat = jnp.maximum(0.0, 1.0 - distance)
                value = value + product[slot * members : (slot + 1) * members] * (hat * hat * valid[slot])
            acc_ref[:, cols] = value
        return carry

    lax.fori_loop(0, (found + GROUP - 1) // GROUP, one_group, 0)
    new_ref[...] = acc_ref[...].astype(jnp.bfloat16)
    if not last:
        following = order_ref[step + 1]
        active = lambda block_id, part: flags_ref[(2 * following + part) * blocks + block_id]
        observe_into(new_ref, tiles_ref, rows_ref, weights_ref, 0, part_ref, keep_ref, send_ref, active, base, half)


def hop(x, axis, flips, size):
    send = lambda bits: lax.ppermute(x, axis, [(j, j ^ bits) for j in range(size)])
    if len(flips) == 1:
        return x + send(flips[0])
    one, two = flips
    a, b, c = send(one), send(two), send(one | two)
    return (x + a) + (b + c)


def shards(
    n_state,
    n_obs,
    prior_state,
    batch_order,
    obs_rows,
    footprint_weights,
    obs_values,
    obs_errors,
    obs_perturbations,
    target_lists,
):
    members, rows_dev = prior_state.shape
    nb, blocks, span = target_lists.shape
    reads, nobs = obs_rows.shape[1:]
    quarter = blocks // 4
    lists = target_lists.reshape(-1)
    half_shape = jax.ShapeDtypeStruct((quarter, members, LANES), jnp.float32)
    state_shape = jax.ShapeDtypeStruct((members, rows_dev), jnp.bfloat16)
    whole2 = lambda i, *refs: (0, 0)
    whole3 = lambda i, *refs: (0, 0, 0)
    batch_of = lambda step: lambda i, order, *refs: (order[step], 0, 0)
    state_spec = pl.BlockSpec((members, rows_dev), whole2)
    half_spec = pl.BlockSpec((quarter, members, LANES), whole3)
    table_spec = pl.BlockSpec((nb, nobs), whole2)
    params = pltpu.CompilerParams(vmem_limit_bytes=48 * 1024 * 1024)
    tile_scratch = [
        pltpu.VMEM((rows_dev // LO, members, LO), jnp.bfloat16),
        pltpu.VMEM((blocks, members, LANES), jnp.float32),
    ]
    reads_specs = lambda step: [pl.BlockSpec((1, reads, nobs), batch_of(step))] * 2

    def reduce_all(keep, send):
        total = keep + lax.ppermute(send, "obs", [(j, j ^ 1) for j in range(n_obs)])
        bit = 2
        while bit < n_obs:
            total = hop(total, "obs", (bit,), n_obs)
            bit *= 2
        bit = 1
        taken = 0
        while bit < n_state:
            if HOPS[taken % len(HOPS)] == 2 and 2 * bit < n_state:
                total = hop(total, "state", (bit, 2 * bit), n_state)
                bit *= 4
            else:
                total = hop(total, "state", (bit,), n_state)
                bit *= 2
            taken += 1
        return total, lax.ppermute(total, "obs", [(j, j ^ 1) for j in range(n_obs)])

    hbm = pl.BlockSpec(memory_space=pltpu.HBM)
    keep, send, flags = pl.pallas_call(
        first_kernel,
        out_shape=(half_shape, half_shape, jax.ShapeDtypeStruct((2 * nb * blocks,), jnp.int32)),
        in_specs=[hbm] * 4,
        out_specs=(pl.BlockSpec(memory_space=pltpu.VMEM),) * 2 + (pl.BlockSpec(memory_space=pltpu.SMEM),),
        scratch_shapes=[
            pltpu.SMEM((nb,), jnp.int32),
            pltpu.VMEM((members, rows_dev), jnp.bfloat16),
            pltpu.VMEM(obs_rows.shape, jnp.int32),
            pltpu.VMEM(obs_rows.shape, jnp.float32),
            *tile_scratch,
            pltpu.SemaphoreType.DMA((4,)),
        ],
        compiler_params=pltpu.CompilerParams(vmem_limit_bytes=62500000),
        name="observe",
    )(batch_order, prior_state, obs_rows, footprint_weights)
    current = prior_state
    for step in range(nb):
        last = step == nb - 1
        own, other = reduce_all(keep, send)
        in_specs = [state_spec, half_spec, half_spec, table_spec, table_spec]
        in_specs += [pl.BlockSpec((1, members, nobs), batch_of(step))]
        args = [batch_order, lists, flags, current, own, other, obs_values, obs_errors, obs_perturbations]
        scratch = [
            pltpu.VMEM((2 * quarter, members, LANES), jnp.float32),
            pltpu.VMEM((members, rows_dev), jnp.float32),
            pltpu.VMEM((GROUP * members, 2 * LANES), jnp.bfloat16),
            pltpu.SMEM((blocks + 1,), jnp.int32),
        ]
        if not last:
            in_specs += reads_specs(step + 1)
            args += [obs_rows, footprint_weights]
            scratch += tile_scratch
        outs = pl.pallas_call(
            functools.partial(step_kernel, blocks, span, step, last),
            out_shape=(state_shape,) if last else (state_shape, half_shape, half_shape),
            grid_spec=pltpu.PrefetchScalarGridSpec(
                num_scalar_prefetch=3,
                grid=(1,),
                in_specs=in_specs,
                out_specs=(state_spec,) if last else (state_spec, half_spec, half_spec),
                scratch_shapes=scratch,
            ),
            compiler_params=params,
            name="last_update" if last else "update_observe",
        )(*args)
        current = outs[0]
        if not last:
            keep, send = outs[1:]
    return current


def solution(mesh):
    return jax.shard_map(
        functools.partial(shards, mesh.shape["state"], mesh.shape["obs"]),
        mesh=mesh,
        in_specs=(P(None, ("state", "obs")), P(), P(), P(), P(), P(), P(), P()),
        out_specs=P(None, ("state", "obs")),
        check_vma=False,
    )
```

```python
import functools
import math

import jax
import jax.numpy as jnp
from jax import lax
from jax.experimental import pallas as pl
from jax.experimental.pallas import tpu as pltpu
from jax.sharding import PartitionSpec as P

OBK = 64
LANES = 128
LO = 256
GROUP = 3
HOPS = (2, 2)
HIGHEST = lax.Precision.HIGHEST
NT = (((1,), (1,)), ((), ()))
TN = (((0,), (0,)), ((), ()))


def touched_blocks(rows_ref, base, rows_dev, flags_ref):
    batches, reads, nobs = rows_ref.shape
    fold = reads // 2
    lane = lax.broadcasted_iota(jnp.int32, (1, LANES), 1)
    read = lax.broadcasted_iota(jnp.int32, (reads, nobs), 0)
    last_pass = jnp.where(read < fold, read, read - fold) >= fold - 2
    bits = 16
    words = [jnp.zeros((1, 1), jnp.float32) for _ in range(2 * batches * nobs // (OBK * bits))]
    place = 0
    for batch in range(batches):
        local = rows_ref[batch] - base
        inside = jnp.where((local >= 0) & (local < rows_dev), 1.0, 0.0)
        for part in (jnp.where(last_pass, 0.0, inside), jnp.where(last_pass, inside, 0.0)):
            hits = jnp.max(part, axis=0, keepdims=True)
            for tile in range(nobs // LANES):
                some = hits[:, tile * LANES : (tile + 1) * LANES]
                for side in (lane < OBK, lane >= OBK):
                    any_hit = jnp.max(jnp.where(side, some, 0.0), axis=1, keepdims=True)
                    words[place // bits] = words[place // bits] + any_hit * float(1 << (place % bits))
                    place += 1
    for at, word in enumerate(words):
        packed = word[0, 0].astype(jnp.int32)
        for bit in range(bits):
            flags_ref[at * bits + bit] = (packed >> bit) & 1


def observe_into(state_ref, tiles_ref, rows_ref, weights_ref, slot, part_ref, keep_ref, send_ref, active, base, half):
    blocks = part_ref.shape[0]
    members = state_ref.shape[0]
    tiles = state_ref.shape[1] // LO
    reads = rows_ref.shape[1]
    fold = reads // 2
    for tile in range(tiles):
        tiles_ref[tile] = state_ref[:, tile * LO : (tile + 1) * LO]
    lane = lax.broadcasted_iota(jnp.int32, (fold, LANES), 1)

    def one_pass(block_id, starts):
        pair = block_id // 2
        odd = block_id - 2 * pair
        lanes = pl.ds(pl.multiple_of(pair * LANES, LANES), LANES)

        def folded(ref):
            top = ref[slot, :fold, lanes]
            bottom = ref[slot, fold:, lanes]
            even = jnp.where(lane < OBK, top, pltpu.roll(bottom, OBK, 1))
            other = jnp.where(lane < OBK, pltpu.roll(top, OBK, 1), bottom)
            return jnp.where(odd == 1, other, even)

        rows = folded(rows_ref) - base
        weights = folded(weights_ref)
        stacked = tiles_ref[...].reshape(tiles * members, LO)
        total = jnp.zeros((members, LANES), jnp.float32)
        for read in starts:
            pick = lambda x: jnp.concatenate([x[read : read + 1], x[read + 1 : read + 2]], axis=1)
            row = pick(rows)
            weight = pick(weights)
            low = row & (LO - 1)
            high = row >> (LO.bit_length() - 1)
            chosen = (lax.broadcasted_iota(jnp.int32, (LO, LO), 0) == low).astype(jnp.float32)
            picked = jnp.dot(stacked, chosen.astype(jnp.bfloat16), preferred_element_type=jnp.float32)
            acc = jnp.zeros((members, LO), jnp.float32)
            for tile in range(tiles):
                scale = jnp.where(high == tile, weight, 0.0)
                acc = acc + picked[tile * members : (tile + 1) * members] * scale
            total = total + (acc[:, :LANES] + acc[:, LANES:])
        part_ref[block_id] += total + pltpu.roll(total, OBK, 1)

    def one_block(block_id, carry):
        part_ref[block_id] = jnp.zeros((members, LANES), jnp.float32)
        for part, starts in enumerate((range(0, fold - 2, 2), (fold - 2,))):
            pl.when(active(block_id, part) != 0)(functools.partial(one_pass, block_id, starts))
        return carry

    lax.fori_loop(0, blocks, one_block, 0)
    low_lane = lax.broadcasted_iota(jnp.int32, (members, LANES), 1) < OBK
    quarter = blocks // 4
    for at in range(quarter):
        for out_ref, side in ((keep_ref, half), (send_ref, 1 - half)):
            first = 2 * (side * quarter + at)
            out_ref[at] = jnp.where(low_lane, part_ref[first], part_ref[first + 1])


def in_two(x):
    coarse = x.astype(jnp.bfloat16)
    return coarse, (x - coarse.astype(jnp.float32)).astype(jnp.bfloat16)


def block_transforms(spreads, misfits, scale):
    obs = spreads[0].shape[0]
    tiles = obs // 8
    groups = range(len(spreads))
    wide = (8, LANES)
    eye = lax.broadcasted_iota(jnp.int32, (obs, obs), 0) == lax.broadcasted_iota(jnp.int32, (obs, obs), 1)
    sublane = lax.broadcasted_iota(jnp.int32, wide, 0)
    split = lambda x: [x[i : i + 8] for i in range(0, obs, 8)]
    row = lambda x, j: jnp.broadcast_to(x[j : j + 1], (8, x.shape[1]))
    system = [
        split(eye.astype(jnp.float32) + lax.dot_general(s, s, NT, precision=HIGHEST, preferred_element_type=jnp.float32))
        for s in spreads
    ]
    right = [split(s) for s in spreads]
    left = [split(m) for m in misfits]
    scaled = [[] for _ in groups]
    for p in range(tiles):
        columns = [
            [[jnp.broadcast_to(system[g][i][:, 8 * p + j : 8 * p + j + 1], wide) for i in range(p, tiles)] for j in range(8)]
            for g in groups
        ]
        factors = [[] for _ in groups]
        inverses = [[] for _ in groups]
        for j in range(8):
            for g in groups:
                panel = columns[g]
                inverse = 1.0 / row(panel[j][0], j)
                factor = [x * inverse for x in panel[j]]
                factor[0] = jnp.where(sublane > j, factor[0], 0.0)
                for k in range(j + 1, 8):
                    pivot_row = row(panel[k][0], j)
                    panel[k] = [x - f * pivot_row for x, f in zip(panel[k], factor)]
                factors[g].append(factor)
                inverses[g].append(inverse)
        for j in range(8):
            for g in groups:
                row_s, row_r, row_l = row(system[g][p], j), row(right[g][p], j), row(left[g][p], j)
                scaled[g].append(right[g][p][j : j + 1] * inverses[g][j][j : j + 1])
                for i in range(p, tiles):
                    if i == p and j == 7:
                        continue
                    factor = factors[g][j][i - p]
                    if i > p or j < 7:
                        system[g][i] = system[g][i] - factor[:, :obs] * row_s
                    right[g][i] = right[g][i] - factor * row_r
                    left[g][i] = left[g][i] - factor * row_l
    results = []
    for g in groups:
        coarse_l, fine_l = in_two(jnp.concatenate(left[g], axis=0))
        coarse_r, fine_r = in_two(jnp.concatenate(scaled[g], axis=0))
        product = lax.dot_general(
            jnp.concatenate([coarse_l, coarse_l, fine_l], axis=0),
            jnp.concatenate([coarse_r, fine_r, coarse_r], axis=0),
            TN,
            preferred_element_type=jnp.float32,
        )
        results.append(product * (1.0 / scale))
    return results


def first_kernel(
    order_hbm,
    state_hbm,
    rows_hbm,
    weights_hbm,
    keep_ref,
    send_ref,
    flags_ref,
    order_ref,
    state_ref,
    rows_ref,
    weights_ref,
    tiles_ref,
    part_ref,
    sems,
):
    pairs = ((rows_hbm, rows_ref), (order_hbm, order_ref), (state_hbm, state_ref), (weights_hbm, weights_ref))
    copies = [pltpu.make_async_copy(a, b, sems.at[i]) for i, (a, b) in enumerate(pairs)]
    for copy in copies:
        copy.start()
    blocks = part_ref.shape[0]
    rows_dev = state_ref.shape[1]
    base = lax.axis_index(("state", "obs")) * rows_dev
    half = lax.axis_index("obs") % 2
    copies[0].wait()
    touched_blocks(rows_ref, base, rows_dev, flags_ref)
    for copy in copies[1:]:
        copy.wait()
    batch = order_ref[0]
    active = lambda block_id, part: flags_ref[(2 * batch + part) * blocks + block_id]
    observe_into(state_ref, tiles_ref, rows_ref, weights_ref, batch, part_ref, keep_ref, send_ref, active, base, half)


def step_kernel(
    blocks,
    span,
    step,
    last,
    order_ref,
    lists_ref,
    flags_ref,
    state_ref,
    own_ref,
    other_ref,
    values_ref,
    errors_ref,
    perturb_ref,
    *rest,
):
    if last:
        new_ref, ens_ref, acc_ref, turn_ref, named_ref = rest
    else:
        rows_ref, weights_ref, new_ref, keep_ref, send_ref, ens_ref, acc_ref, turn_ref, named_ref = rest[:9]
        tiles_ref, part_ref = rest[9:]
    members, rows_dev = state_ref.shape
    shard_id = lax.axis_index(("state", "obs"))
    half = lax.axis_index("obs") % 2
    base = shard_id * rows_dev
    batch = order_ref[step]
    quarter = blocks // 4
    scale = math.sqrt(members - 1)
    reach_rows = span * rows_dev // 2

    ens_ref[pl.ds(half * quarter, quarter)] = own_ref[...]
    ens_ref[pl.ds((1 - half) * quarter, quarter)] = other_ref[...]

    def scan(block_id, found):
        begin = (batch * blocks + block_id) * span
        look = lambda slot, hit: hit | (lists_ref[begin + slot] == shard_id).astype(jnp.int32)
        named_ref[found] = block_id
        return found + lax.fori_loop(0, span, look, jnp.int32(0))

    found = lax.fori_loop(0, blocks, scan, jnp.int32(0))

    def transposed(place):
        block_id = named_ref[place]
        pair = block_id // 2
        odd = block_id - 2 * pair
        ens = ens_ref[pair]
        lanes = pl.ds(pl.multiple_of(pair * LANES, LANES), LANES)
        mine = lax.broadcasted_iota(jnp.int32, (values_ref.shape[0], LANES), 0) == batch
        of_batch = lambda ref: jnp.sum(jnp.where(mine, ref[:, lanes], 0.0), axis=0, keepdims=True)
        error = of_batch(errors_ref)
        value = of_batch(values_ref)
        pert = perturb_ref[0, :, lanes]
        mean = jnp.sum(ens, axis=0, keepdims=True) * (1.0 / members)
        spread = (ens - mean) * (1.0 / (error * scale))
        misfit = (value + error * pert - ens) * (1.0 / error)
        pad = jnp.zeros((LANES - members, LANES), jnp.float32)
        turn = lambda x: jnp.concatenate([x, pad], axis=0).T
        pick = lambda x: jnp.where(odd == 1, x[OBK:], x[:OBK])
        return pick(turn(spread)), pick(turn(misfit))

    tiles = rows_dev // LO
    turn_ref[...] = jnp.zeros(turn_ref.shape, jnp.bfloat16)
    acc_ref[...] = state_ref[...].astype(jnp.float32)

    def one_group(group, carry):
        first = group * GROUP
        for size in range(1, GROUP + 1):

            @pl.when(jnp.minimum(found - first, GROUP) == size)
            def _(size=size):
                sides = [transposed(first + slot) for slot in range(size)]
                results = block_transforms([s for s, _ in sides], [m for _, m in sides], scale)
                blank = jnp.zeros((members, LANES), jnp.float32)
                for slot, result in enumerate(results):
                    result = result[:members]
                    centred = result - jnp.sum(result, axis=1, keepdims=True) * (1.0 / members)
                    centred = jnp.where(lax.broadcasted_iota(jnp.int32, centred.shape, 1) < members, centred, 0.0)
                    coarse, fine = (x.astype(jnp.float32) for x in in_two(centred))
                    beside = pltpu.roll(jnp.concatenate([fine, blank], axis=1), members, 1)
                    beside = beside + jnp.concatenate([coarse, blank], axis=1)
                    turn_ref[slot * members : (slot + 1) * members] = beside.astype(jnp.bfloat16)

        centres, valid = [], []
        for slot in range(GROUP):
            place = jnp.minimum(first + slot, found - 1)
            centres.append(lists_ref[(batch * blocks + named_ref[place]) * span] * rows_dev + rows_dev // 2)
            valid.append((first + slot < found).astype(jnp.float32))
        for tile in range(tiles):
            cols = slice(tile * LO, (tile + 1) * LO)
            twice = jnp.concatenate([state_ref[:, cols]] * 2, axis=0)
            product = jnp.dot(turn_ref[:, : 2 * members], twice, preferred_element_type=jnp.float32)
            value = acc_ref[:, cols]
            positions = base + tile * LO + lax.broadcasted_iota(jnp.int32, (1, LO), 1)
            for slot in range(GROUP):
                distance = jnp.abs(positions - centres[slot]).astype(jnp.float32) / reach_rows
                hat = jnp.maximum(0.0, 1.0 - distance)
                value = value + product[slot * members : (slot + 1) * members] * (hat * hat * valid[slot])
            acc_ref[:, cols] = value
        return carry

    lax.fori_loop(0, (found + GROUP - 1) // GROUP, one_group, 0)
    new_ref[...] = acc_ref[...].astype(jnp.bfloat16)
    if not last:
        following = order_ref[step + 1]
        active = lambda block_id, part: flags_ref[(2 * following + part) * blocks + block_id]
        observe_into(new_ref, tiles_ref, rows_ref, weights_ref, 0, part_ref, keep_ref, send_ref, active, base, half)


def hop(x, axis, flips, size):
    send = lambda bits: lax.ppermute(x, axis, [(j, j ^ bits) for j in range(size)])
    if len(flips) == 1:
        return x + send(flips[0])
    one, two = flips
    a, b, c = send(one), send(two), send(one | two)
    return (x + a) + (b + c)


def shards(
    n_state,
    n_obs,
    prior_state,
    batch_order,
    obs_rows,
    footprint_weights,
    obs_values,
    obs_errors,
    obs_perturbations,
    target_lists,
):
    members, rows_dev = prior_state.shape
    nb, blocks, span = target_lists.shape
    reads, nobs = obs_rows.shape[1:]
    quarter = blocks // 4
    lists = target_lists.reshape(-1)
    half_shape = jax.ShapeDtypeStruct((quarter, members, LANES), jnp.float32)
    state_shape = jax.ShapeDtypeStruct((members, rows_dev), jnp.bfloat16)
    whole2 = lambda i, *refs: (0, 0)
    whole3 = lambda i, *refs: (0, 0, 0)
    batch_of = lambda step: lambda i, order, *refs: (order[step], 0, 0)
    state_spec = pl.BlockSpec((members, rows_dev), whole2)
    half_spec = pl.BlockSpec((quarter, members, LANES), whole3)
    table_spec = pl.BlockSpec((nb, nobs), whole2)
    params = pltpu.CompilerParams(vmem_limit_bytes=48 * 1024 * 1024)
    tile_scratch = [
        pltpu.VMEM((rows_dev // LO, members, LO), jnp.bfloat16),
        pltpu.VMEM((blocks, members, LANES), jnp.float32),
    ]
    reads_specs = lambda step: [pl.BlockSpec((1, reads, nobs), batch_of(step))] * 2

    def reduce_all(keep, send):
        total = keep + lax.ppermute(send, "obs", [(j, j ^ 1) for j in range(n_obs)])
        bit = 2
        while bit < n_obs:
            total = hop(total, "obs", (bit,), n_obs)
            bit *= 2
        bit = 1
        taken = 0
        while bit < n_state:
            if HOPS[taken % len(HOPS)] == 2 and 2 * bit < n_state:
                total = hop(total, "state", (bit, 2 * bit), n_state)
                bit *= 4
            else:
                total = hop(total, "state", (bit,), n_state)
                bit *= 2
            taken += 1
        return total, lax.ppermute(total, "obs", [(j, j ^ 1) for j in range(n_obs)])

    hbm = pl.BlockSpec(memory_space=pltpu.HBM)
    keep, send, flags = pl.pallas_call(
        first_kernel,
        out_shape=(half_shape, half_shape, jax.ShapeDtypeStruct((2 * nb * blocks,), jnp.int32)),
        in_specs=[hbm] * 4,
        out_specs=(pl.BlockSpec(memory_space=pltpu.VMEM),) * 2 + (pl.BlockSpec(memory_space=pltpu.SMEM),),
        scratch_shapes=[
            pltpu.SMEM((nb,), jnp.int32),
            pltpu.VMEM((members, rows_dev), jnp.bfloat16),
            pltpu.VMEM(obs_rows.shape, jnp.int32),
            pltpu.VMEM(obs_rows.shape, jnp.float32),
            *tile_scratch,
            pltpu.SemaphoreType.DMA((4,)),
        ],
        compiler_params=pltpu.CompilerParams(vmem_limit_bytes=62500000),
        name="observe",
    )(batch_order, prior_state, obs_rows, footprint_weights)
    current = prior_state
    for step in range(nb):
        last = step == nb - 1
        own, other = reduce_all(keep, send)
        in_specs = [state_spec, half_spec, half_spec, table_spec, table_spec]
        in_specs += [pl.BlockSpec((1, members, nobs), batch_of(step))]
        args = [batch_order, lists, flags, current, own, other, obs_values, obs_errors, obs_perturbations]
        scratch = [
            pltpu.VMEM((2 * quarter, members, LANES), jnp.float32),
            pltpu.VMEM((members, rows_dev), jnp.float32),
            pltpu.VMEM((GROUP * members, 2 * LANES), jnp.bfloat16),
            pltpu.SMEM((blocks + 1,), jnp.int32),
        ]
        if not last:
            in_specs += reads_specs(step + 1)
            args += [obs_rows, footprint_weights]
            scratch += tile_scratch
        outs = pl.pallas_call(
            functools.partial(step_kernel, blocks, span, step, last),
            out_shape=(state_shape,) if last else (state_shape, half_shape, half_shape),
            grid_spec=pltpu.PrefetchScalarGridSpec(
                num_scalar_prefetch=3,
                grid=(1,),
                in_specs=in_specs,
                out_specs=(state_spec,) if last else (state_spec, half_spec, half_spec),
                scratch_shapes=scratch,
            ),
            compiler_params=params,
            name="last_update" if last else "update_observe",
        )(*args)
        current = outs[0]
        if not last:
            keep, send = outs[1:]
    return current


def solution(mesh):
    return jax.shard_map(
        functools.partial(shards, mesh.shape["state"], mesh.shape["obs"]),
        mesh=mesh,
        in_specs=(P(None, ("state", "obs")), P(), P(), P(), P(), P(), P(), P()),
        out_specs=P(None, ("state", "obs")),
        check_vma=False,
    )
```
